256 devices in a mesh: tm: 64 (over z_lo, x, y, core), tensor: 4 (over z_hi).
Axes of the slice: x: 4, y: 4, z: 8 (z_hi: 4, z_lo: 2; z = z_hi * 2 + z_lo), core: 2. Of those that a mesh axis runs over, the one named last changes fastest.
Arguments:
- inputs: bfloat16 [131072, 1536], P('tm', 'tensor'), may hold values from -6 to 6
- kernel: bfloat16 [131072, 1536], P('tm', 'tensor'), may hold values from -5 to 5
- w_in: bfloat16 [12, 128, 128], P('tensor'), may hold values from -0.5 to 0.5
- w_gate: bfloat16 [12, 128, 128], P('tensor'), may hold values from -0.5 to 0.5
- w_out: bfloat16 [12, 128, 128], P('tensor'), may hold values from -0.5 to 0.5
- factor_a: bfloat16 [512, 512], replicated, may hold values from -0.25 to 0.25
- factor_b: bfloat16 [256, 256], replicated, may hold values from -0.375 to 0.375
- cotangent: bfloat16 [131072, 1536], P('tm', 'tensor'), may hold values from -6 to 6
Outputs:
- outputs: bfloat16 [131072, 1536], P('tm', 'tensor')
- grad_inputs: bfloat16 [131072, 1536], P('tm', 'tensor')
- grad_kernel: bfloat16 [131072, 1536], P('tm', 'tensor')
- grad_w_in: float32 [12, 128, 128], P('tensor')
- grad_w_gate: float32 [12, 128, 128], P('tensor')
- grad_w_out: float32 [12, 128, 128], P('tensor')
- grad_factor_a: float32 [512, 512], P('tm')
- grad_factor_b: float32 [256, 256], P('tm')
The draws below stay inside these ranges and needn't reach their ends.
All inputs are finite; a program needn't handle non-finite values.
Results may differ from the reference program's by a relative error of at most 0.0071.
Values may be sent and summed in bfloat16 or wider, within the bound.
A program may use at most 128 MiB of HBM per device.

```python
import math
import jax
import jax.numpy as jnp

D = 1536
BLOCK = 128
N1 = 256
N2 = 512
LENGTH = 131072
NBLOCKS = 12


def steps_of(rng, extent, cuts, smallest, top_value):
    def one(dim, shards_of):
        heights = jax.random.uniform(jax.random.fold_in(jax.random.fold_in(rng, 6), dim), (shards_of,), jnp.float32, smallest / len(cuts), top_value / len(cuts))
        return jnp.repeat(jnp.exp(heights), extent[dim] // shards_of).reshape((-1,) + (1,) * (len(extent) - dim - 1))

    level = one(*cuts[0])
    for cut in cuts[1:]:
        level = level * one(*cut)
    return level


def gaussian(key, dims, spread, limit, cuts=(), dtype=jnp.bfloat16):
    values = spread * jax.random.normal(key, dims, jnp.float32)
    if cuts:
        values = values * steps_of(key, dims, cuts, -0.22, 0.18)
    return jnp.clip(values, -limit, limit).astype(dtype)


def setup_inputs(seed: int = 0) -> dict:
    key_of = jax.random.split(jax.random.key(seed), 9)
    inputs = gaussian(key_of[0], (LENGTH, D), 1.0, 6.0, ((0, 64), (1, 4)))
    kernel = gaussian(key_of[1], (LENGTH, D), 1.0, 5.0, ((0, 64), (1, 4)))
    w_in = gaussian(key_of[2], (NBLOCKS, BLOCK, BLOCK), BLOCK ** -0.5, 0.5, ((0, 4),))
    w_gate = gaussian(key_of[3], (NBLOCKS, BLOCK, BLOCK), BLOCK ** -0.5, 0.5, ((0, 4),))
    w_out = gaussian(key_of[4], (NBLOCKS, BLOCK, BLOCK), BLOCK ** -0.5, 0.5, ((0, 4),))
    factor_a = gaussian(key_of[5], (N2, N2), N2 ** -0.5, 0.25)
    factor_b = gaussian(key_of[6], (N1, N1), N1 ** -0.5, 0.375)
    cotangent = gaussian(key_of[7], (LENGTH, D), 1.0, 6.0, ((0, 64), (1, 4)))
    return {"inputs": inputs, "kernel": kernel, "w_in": w_in, "w_gate": w_gate, "w_out": w_out, "factor_a": factor_a, "factor_b": factor_b, "cotangent": cotangent}


def mix(act, weight):
    blocks = act.reshape(act.shape[0], D // BLOCK, BLOCK).astype(jnp.float32)
    out = jnp.einsum('tnb,nbe->tne', blocks, weight.astype(jnp.float32))
    return out.reshape(act.shape[0], D)

def mix_back(grad, weight):
    blocks = grad.reshape(grad.shape[0], D // BLOCK, BLOCK).astype(jnp.float32)
    out = jnp.einsum('tne,nbe->tnb', blocks, weight.astype(jnp.float32))
    return out.reshape(grad.shape[0], D)

def mix_grad(act, grad):
    left = act.reshape(act.shape[0], D // BLOCK, BLOCK).astype(jnp.float32)
    right = grad.reshape(grad.shape[0], D // BLOCK, BLOCK).astype(jnp.float32)
    return jnp.einsum('tnb,tne->nbe', left, right) / math.sqrt(N1 * N2)

def reference(inputs, kernel, w_in, w_gate, w_out, factor_a, factor_b, cotangent):
    fa = factor_a.astype(jnp.float32)
    fb = factor_b.astype(jnp.float32)
    mixed_in = mix(inputs, w_in).astype(jnp.bfloat16)
    gate = mix(inputs, w_gate)
    mixed3 = mixed_in.reshape(N1, N2, D)
    first = jnp.einsum('ijc,jk->ikc', mixed3.astype(jnp.float32), fa)
    twiddle = kernel.reshape(N1, N2, D).astype(jnp.float32)
    twisted = (first * twiddle).astype(jnp.bfloat16)
    second = jnp.einsum('im,ikc->mkc', fb, twisted.astype(jnp.float32)).astype(jnp.bfloat16)
    second = second.reshape(N1 * N2, D)
    gated = (second.astype(jnp.float32) * gate).astype(jnp.bfloat16)
    outputs = mix(gated, w_out).astype(jnp.bfloat16)
    grad_gated = mix_back(cotangent, w_out)
    grad_second = (grad_gated * gate).astype(jnp.bfloat16)
    grad_gate = (grad_gated * second.astype(jnp.float32)).astype(jnp.bfloat16)
    grad_second3 = grad_second.reshape(N1, N2, D).astype(jnp.float32)
    grad_twisted = jnp.einsum('im,mkc->ikc', fb, grad_second3).astype(jnp.bfloat16)
    grad_factor_b = jnp.einsum('ikc,mkc->im', twisted.astype(jnp.float32), grad_second3) / math.sqrt(N2 * D)
    grad_tw32 = grad_twisted.astype(jnp.float32)
    grad_first = (grad_tw32 * twiddle).astype(jnp.bfloat16)
    grad_kernel = (grad_tw32 * first).astype(jnp.bfloat16).reshape(N1 * N2, D)
    grad_first32 = grad_first.astype(jnp.float32)
    grad_factor_a = jnp.einsum('ijc,ikc->jk', mixed3.astype(jnp.float32), grad_first32) / math.sqrt(N1 * D)
    grad_mixed = jnp.einsum('jk,ikc->ijc', fa, grad_first32).astype(jnp.bfloat16).reshape(N1 * N2, D)
    grad_inputs = (mix_back(grad_mixed, w_in) + mix_back(grad_gate, w_gate)).astype(jnp.bfloat16)
    grad_w_in = mix_grad(inputs, grad_mixed)
    grad_w_gate = mix_grad(inputs, grad_gate)
    grad_w_out = mix_grad(gated, cotangent)
    return (outputs, grad_inputs, grad_kernel, grad_w_in, grad_w_gate, grad_w_out, grad_factor_a, grad_factor_b)
```

```python
import math

import jax
import jax.numpy as jnp
from jax import lax
from jax.experimental import pallas as pl
from jax.experimental.pallas import tpu as pltpu
from jax.sharding import PartitionSpec as P

D = 1536
N1 = 256
N2 = 512
MESH = pl.DeviceIdType.MESH
F32 = jnp.float32
BF16 = jnp.bfloat16
TM = 64
TE = 4
ROWS = 2048
CH = 384
LOC = 4
KD = 8
NB = 3
DC = 8
CR = DC * KD


def lanes(n):
    return slice(n * 128, (n + 1) * 128)


def nt(a, b):
    return lax.dot_general(a, b, (((1,), (1,)), ((), ())), preferred_element_type=F32)


def nn(a, b):
    return jnp.dot(a, b, preferred_element_type=F32)


def four(ref, c, n):
    return jnp.concatenate(
        [ref[pl.ds(i * N2 + c * CR, CR), lanes(n)] for i in range(LOC)], axis=0
    )


def put_four(ref, c, n, val):
    for i in range(LOC):
        ref[pl.ds(i * N2 + c * CR, CR), lanes(n)] = val[i * CR : (i + 1) * CR]


def by_dest(val):
    return jnp.concatenate(
        [
            val[i * CR + d * KD : i * CR + (d + 1) * KD]
            for d in range(DC)
            for i in range(LOC)
        ],
        axis=0,
    )


def by_block(val):
    return jnp.concatenate(
        [
            val[(d * LOC + i) * KD : (d * LOC + i + 1) * KD]
            for i in range(LOC)
            for d in range(DC)
        ],
        axis=0,
    )


def kernel_body(
    in_h,
    ker_h,
    w_in,
    w_gate,
    w_out,
    fa,
    fb,
    cot_h,
    out_h,
    gin_h,
    gker_h,
    gw_in,
    gw_gate,
    gw_out,
    gfa,
    gfb,
    in_v,
    ker_v,
    cot_v,
    in_t,
    cot_t,
    a_t,
    b_t,
    gate_v,
    gg_v,
    first_v,
    mx_v,
    so_g,
    so_f,
    rc_g,
    rc_f,
    xs,
    x_g,
    x_f,
    sr_g,
    sr_f,
    rr_g,
    rr_f,
    gf_v,
    gm_v,
    gated_v,
    ggate_v,
    out_v,
    gin_v,
    gker_v,
    fb_acc,
    fa_acc,
    r1s,
    r1r,
    r2s,
    r2r,
    tr,
    pr,
    ag1,
    ag2,
    ld_sem,
    st_sem,
    snd,
    rcv,
):
    me = lax.axis_index("tm")
    te = lax.axis_index("tensor")
    core = lax.rem(me, 2)
    my = lax.rem(me // 2, 4)
    mx = lax.rem(me // 8, 4)
    mz = me // 32

    def peer(p):
        o = lax.rem((p - 1) * 37, 63) + 1
        dc = lax.rem(core + lax.rem(o, 2), 2)
        dy = lax.rem(my + lax.rem(o // 2, 4), 4)
        dx = lax.rem(mx + lax.rem(o // 8, 4), 4)
        dz = lax.rem(mz + o // 32, 2)
        return ((dz * 4 + dx) * 4 + dy) * 2 + dc

    loads = [
        pltpu.make_async_copy(cot_h, cot_v, ld_sem.at[0]),
        pltpu.make_async_copy(in_h, in_v, ld_sem.at[1]),
        pltpu.make_async_copy(ker_h, ker_v, ld_sem.at[2]),
    ]
    for cp in loads:
        cp.start()

    barrier = pltpu.get_barrier_semaphore()

    @pl.loop(1, TM)
    def _(p):
        pl.semaphore_signal(barrier, inc=1, device_id=(peer(p), te), device_id_type=MESH)

    for q in range(1, TE):
        pl.semaphore_signal(
            barrier, inc=1, device_id=(me, lax.rem(te + q, TE)), device_id_type=MESH
        )

    def copy_to(src, dst, ph, device):
        return pltpu.make_async_remote_copy(
            src_ref=src,
            dst_ref=dst,
            send_sem=snd.at[ph],
            recv_sem=rcv.at[ph],
            device_id=device,
            device_id_type=MESH,
        )

    def send_all(slot_of, dst, ph):
        @pl.loop(1, TM)
        def _(p):
            d = peer(p)
            copy_to(slot_of(d), dst.at[me], ph, (d, te)).start()

    def wait_slots(ref, sem, slots=TM - 1):
        part = ref.at[pl.ds(0, slots)]
        pltpu.make_async_copy(part, part, sem).wait()

    loads[0].wait()
    loads[1].wait()

    @pl.loop(0, N2 // CR)
    def _(c):
        for n in range(NB):
            gate = nn(four(in_v, c, n), w_gate[n])
            gg = nt(four(cot_v, c, n), w_out[n])
            put_four(gate_v, c, n, gate)
            put_four(gg_v, c, n, gg)
            so_g[pl.ds(c * DC, DC), :, lanes(n)] = (
                by_dest(gate * gg).astype(BF16).reshape(DC, LOC * KD, 128)
            )

    pl.semaphore_wait(barrier, TM - 1 + TE - 1)
    send_all(lambda d: so_g.at[d], rc_g, 0)

    for s in range(4):
        a_t[:, lanes(s)] = fa[lanes(s), :].T

    @pl.loop(0, LOC)
    def _(i):
        rows = pl.ds(pl.multiple_of(i * N2, N2), N2)
        for n in range(NB):
            mx_v[rows, lanes(n)] = nn(in_v[rows, lanes(n)], w_in[n]).astype(BF16)
        first_v[rows, :] = nn(a_t[...], mx_v[rows, :])

    loads[2].wait()

    @pl.loop(0, N2 // CR)
    def _(c):
        for n in range(NB):
            tw = four(first_v, c, n) * four(ker_v, c, n).astype(F32)
            so_f[pl.ds(c * DC, DC), :, lanes(n)] = (
                by_dest(tw).astype(BF16).reshape(DC, LOC * KD, 128)
            )

    send_all(lambda d: so_f.at[d], rc_f, 1)
    rc_g[me] = so_g[me]
    rc_f[me] = so_f[me]

    b_t[...] = fb[...].T

    @pl.loop(0, ROWS // 256)
    def _(c):
        rows = pl.ds(pl.multiple_of(c * 256, 256), 256)
        for n in range(NB):
            in_t[n, :, rows] = in_v[rows, lanes(n)].T
            cot_t[n, :, rows] = cot_v[rows, lanes(n)].T

    def columns(rc, x):
        @pl.loop(0, 8)
        def _(c):
            rows = pl.ds(pl.multiple_of(c * 256, 256), 256)
            for n in range(NB):
                xs[n, rows, :] = rc[pl.ds(c * 8, 8), :, lanes(n)].reshape(256, 128).astype(F32)

        for k in range(KD):
            for n in range(NB):
                x[k, :, lanes(n)] = xs[n, pl.ds(k, N1, stride=KD), :].astype(BF16)

    def product(lhs, x, sr):
        for k in range(KD):
            y = nn(lhs[...], x[k])
            for n in range(NB):
                xs[n, pl.ds(k, N1, stride=KD), :] = y[:, lanes(n)]

        @pl.loop(0, 8)
        def _(c):
            rows = pl.ds(pl.multiple_of(c * 256, 256), 256)
            for n in range(NB):
                sr[pl.ds(c * 8, 8), :, lanes(n)] = (
                    xs[n, rows, :].astype(BF16).reshape(8, LOC * KD, 128)
                )

    wait_slots(rc_g, rcv.at[0])
    columns(rc_g, x_g)
    product(fb, x_g, sr_g)
    send_all(lambda d: sr_g.at[d], rr_g, 2)
    rr_g[me] = sr_g[me]

    wait_slots(rc_f, rcv.at[1])
    columns(rc_f, x_f)
    product(b_t, x_f, sr_f)
    send_all(lambda d: sr_f.at[d], rr_f, 3)
    rr_f[me] = sr_f[me]

    fb_acc[...] = nt(x_f[0], x_g[0])

    @pl.loop(1, KD)
    def _(k):
        fb_acc[...] += nt(x_f[k], x_g[k])

    for h in range(2):
        r1s[:, h, :, 512:640] = fb_acc[:, lanes(h)].reshape(TM // 2, 8, 128)

    wait_slots(rr_g, rcv.at[2])

    @pl.loop(0, N2 // CR)
    def _(c):
        for n in range(NB):
            gt = by_block(
                rr_g[pl.ds(c * DC, DC), :, lanes(n)].reshape(LOC * CR, 128).astype(F32)
            )
            gf = (gt * four(ker_v, c, n).astype(F32)).astype(BF16)
            gk = (gt * four(first_v, c, n)).astype(BF16)
            put_four(gf_v, c, n, gf)
            put_four(gker_v, c, n, gk)

    stores = [
        pltpu.make_async_copy(gker_v, gker_h, st_sem.at[0]),
        pltpu.make_async_copy(out_v, out_h, st_sem.at[1]),
        pltpu.make_async_copy(gin_v, gin_h, st_sem.at[2]),
    ]
    stores[0].start()

    fa_acc[...] = jnp.zeros_like(fa_acc)

    @pl.loop(0, LOC)
    def _(i):
        rows = pl.ds(pl.multiple_of(i * N2, N2), N2)
        gm_v[rows, :] = nn(fa[...], gf_v[rows, :]).astype(BF16)
        fa_acc[...] += nt(mx_v[rows, :], gf_v[rows, :])

    r1s[:, :, :, 0:512] = fa_acc[...].reshape(TM // 2, 2, 8, 512)
    for n in range(NB):
        r1s[n * 8 : (n + 1) * 8, :, :, 640:768] = nn(in_t[n], gm_v[:, lanes(n)]).reshape(
            8, 2, 8, 128
        )
    r1s[24:32, :, :, 640:768] = jnp.zeros((8, 2, 8, 128), F32)
    send_all(lambda d: r1s.at[d // 2, lax.rem(d, 2)], r1r, 4)
    r1r[me] = r1s[me // 2, core]

    wait_slots(rr_f, rcv.at[3])

    @pl.loop(0, N2 // CR)
    def _(c):
        for n in range(NB):
            sec = by_block(
                rr_f[pl.ds(c * DC, DC), :, lanes(n)].reshape(LOC * CR, 128).astype(F32)
            )
            put_four(gated_v, c, n, (sec * four(gate_v, c, n)).astype(BF16))
            put_four(ggate_v, c, n, (sec * four(gg_v, c, n)).astype(BF16))

    for n in range(NB):
        r2s[n * 16 : (n + 1) * 16, 0] = nn(in_t[n], ggate_v[:, lanes(n)]).reshape(16, 8, 128)
        r2s[n * 16 : (n + 1) * 16, 1] = nn(cot_t[n], gated_v[:, lanes(n)]).T.reshape(16, 8, 128)
    r2s[48:64] = jnp.zeros((16, 2, 8, 128), F32)
    send_all(lambda d: r2s.at[d], r2r, 7)
    r2r[me] = r2s[me]

    @pl.loop(0, ROWS // 256)
    def _(c):
        rows = pl.ds(pl.multiple_of(c * 256, 256), 256)
        for n in range(NB):
            out_v[rows, lanes(n)] = nn(gated_v[rows, lanes(n)], w_out[n]).astype(BF16)
            gin_v[rows, lanes(n)] = (
                nt(gm_v[rows, lanes(n)], w_in[n]) + nt(ggate_v[rows, lanes(n)], w_gate[n])
            ).astype(BF16)

    stores[1].start()
    stores[2].start()

    token_scale = 1.0 / math.sqrt(N1 * N2)
    wait_slots(r1r, rcv.at[4])
    sum1 = lax.fori_loop(1, TM, lambda q, acc: acc + r1r[q], r1r[0])
    tr[te] = sum1[:, 0:640]
    for q in range(1, TE):
        copy_to(tr.at[te], tr.at[te], 5, (me, lax.rem(te + q, TE))).start()
    ag1[me] = sum1[:, 640:768] * token_scale
    send_all(lambda d: ag1.at[me], ag1, 8)

    wait_slots(r2r, rcv.at[7])
    sum2 = lax.fori_loop(1, TM, lambda q, acc: acc + r2r[q], r2r[0])
    ag2[me] = sum2 * token_scale
    send_all(lambda d: ag2.at[me], ag2, 9)

    wait_slots(tr, rcv.at[5], TE - 1)
    total = tr[0] + tr[1] + tr[2] + tr[3]
    gfa[...] = total[:, 0:512] * (1.0 / math.sqrt(N1 * D))
    pr[core] = total[:, 512:640] * (1.0 / math.sqrt(N2 * D))
    pair = copy_to(pr.at[core], pr.at[core], 6, (me + 1 - 2 * core, te))
    pair.start()
    pair.wait()
    for h in range(2):
        gfb[:, lanes(h)] = jnp.where(core == 0, pr[h, 0:4, :], pr[h, 4:8, :])

    wait_slots(ag1, rcv.at[8])
    gw_in[...] = ag1[0:48]
    wait_slots(ag2, rcv.at[9])
    gw_gate[...] = ag2[0:48, 0]
    gw_out[...] = ag2[0:48, 1]

    wait_slots(rc_g, snd.at[0])
    wait_slots(rc_f, snd.at[1])
    wait_slots(rr_g, snd.at[2])
    wait_slots(rr_f, snd.at[3])
    wait_slots(r1r, snd.at[4])
    wait_slots(tr, snd.at[5], TE - 1)
    wait_slots(r2r, snd.at[7])
    wait_slots(ag1, snd.at[8])
    wait_slots(ag2, snd.at[9])
    for cp in stores:
        cp.wait()


def body(inputs, kernel, w_in, w_gate, w_out, factor_a, factor_b, cotangent):
    any_spec = pl.BlockSpec(memory_space=pl.ANY)
    vm = pl.BlockSpec(memory_space=pltpu.VMEM)
    big = jax.ShapeDtypeStruct((ROWS, CH), BF16)
    wide = pltpu.VMEM((ROWS, CH), F32)
    act = pltpu.VMEM((ROWS, CH), BF16)
    turned = pltpu.VMEM((NB, 128, ROWS), BF16)
    slots = pltpu.VMEM((TM, LOC * KD, CH), BF16)
    cols = pltpu.VMEM((KD, N1, CH), BF16)
    tile = jax.ShapeDtypeStruct((48, 8, 128), F32)
    outs = pl.pallas_call(
        kernel_body,
        name="monarch",
        out_shape=(
            big,
            big,
            big,
            tile,
            tile,
            tile,
            jax.ShapeDtypeStruct((8, N2), F32),
            jax.ShapeDtypeStruct((4, N1), F32),
        ),
        in_specs=[any_spec, any_spec, vm, vm, vm, vm, vm, any_spec],
        out_specs=(any_spec, any_spec, any_spec, vm, vm, vm, vm, vm),
        scratch_shapes=[
            act,
            act,
            act,
            turned,
            turned,
            pltpu.VMEM((N2, N2), BF16),
            pltpu.VMEM((N1, N1), BF16),
            wide,
            wide,
            wide,
            act,
            slots,
            slots,
            slots,
            slots,
            pltpu.VMEM((NB, ROWS, 128), F32),
            cols,
            cols,
            slots,
            slots,
            slots,
            slots,
            act,
            act,
            act,
            act,
            act,
            act,
            act,
            pltpu.VMEM((N1, N1), F32),
            pltpu.VMEM((N2, N2), F32),
            pltpu.VMEM((TM // 2, 2, 8, 768), F32),
            pltpu.VMEM((TM, 8, 768), F32),
            pltpu.VMEM((TM, 2, 8, 128), F32),
            pltpu.VMEM((TM, 2, 8, 128), F32),
            pltpu.VMEM((TE, 8, 640), F32),
            pltpu.VMEM((2, 8, 128), F32),
            pltpu.VMEM((TM, 8, 128), F32),
            pltpu.VMEM((TM, 2, 8, 128), F32),
            pltpu.SemaphoreType.DMA((3,)),
            pltpu.SemaphoreType.DMA((3,)),
            pltpu.SemaphoreType.DMA((10,)),
            pltpu.SemaphoreType.DMA((10,)),
        ],
        compiler_params=pltpu.CompilerParams(
            collective_id=0, has_side_effects=True, vmem_limit_bytes=67043328
        ),
    )(inputs, kernel, w_in, w_gate, w_out, factor_a, factor_b, cotangent)
    out, gin, gker, gwi, gwg, gwo, gfa, gfb = outs
    shape = (NB, 128, 128)
    return (
        out,
        gin,
        gker,
        gwi.reshape(shape),
        gwg.reshape(shape),
        gwo.reshape(shape),
        gfa,
        gfb,
    )


def solution(mesh):
    return jax.shard_map(
        body,
        mesh=mesh,
        in_specs=(
            P("tm", "tensor"),
            P("tm", "tensor"),
            P("tensor", None, None),
            P("tensor", None, None),
            P("tensor", None, None),
            P(),
            P(),
            P("tm", "tensor"),
        ),
        out_specs=(
            P("tm", "tensor"),
            P("tm", "tensor"),
            P("tm", "tensor"),
            P("tensor", None, None),
            P("tensor", None, None),
            P("tensor", None, None),
            P("tm", None),
            P("tm", None),
        ),
        check_vma=False,
    )
```

```python
import math

import jax
import jax.numpy as jnp
from jax import lax
from jax.experimental import pallas as pl
from jax.experimental.pallas import tpu as pltpu
from jax.sharding import PartitionSpec as P

D = 1536
N1 = 256
N2 = 512
MESH = pl.DeviceIdType.MESH
F32 = jnp.float32
BF16 = jnp.bfloat16
TM = 64
TE = 4
ROWS = 2048
CH = 384
LOC = 4
KD = 8
NB = 3
OWN = 48
DC = 8
CR = DC * KD


def lanes(n):
    return slice(n * 128, (n + 1) * 128)


def nt(a, b):
    return lax.dot_general(a, b, (((1,), (1,)), ((), ())), preferred_element_type=F32)


def nn(a, b):
    return jnp.dot(a, b, preferred_element_type=F32)


def four(ref, c, n):
    return jnp.concatenate(
        [ref[pl.ds(i * N2 + c * CR, CR), lanes(n)] for i in range(LOC)], axis=0
    )


def put_four(ref, c, n, val):
    for i in range(LOC):
        ref[pl.ds(i * N2 + c * CR, CR), lanes(n)] = val[i * CR : (i + 1) * CR]


def by_dest(val):
    return jnp.concatenate(
        [
            val[i * CR + d * KD : i * CR + (d + 1) * KD]
            for d in range(DC)
            for i in range(LOC)
        ],
        axis=0,
    )


def by_block(val):
    return jnp.concatenate(
        [
            val[(d * LOC + i) * KD : (d * LOC + i + 1) * KD]
            for i in range(LOC)
            for d in range(DC)
        ],
        axis=0,
    )


def kernel_body(
    in_h,
    ker_h,
    w_in,
    w_gate,
    w_out,
    fa,
    fb,
    cot_h,
    out_v,
    gin_v,
    gker_v,
    gw_in,
    gw_gate,
    gw_out,
    gfa,
    gfb,
    in_v,
    ker_v,
    cot_v,
    in_t,
    cot_t,
    a_t,
    b_t,
    gate_v,
    gg_v,
    first_v,
    mx_v,
    so_g,
    so_f,
    rc_g,
    rc_f,
    xs,
    x_g,
    x_f,
    sr_g,
    sr_f,
    rr_g,
    rr_f,
    gf_v,
    gm_v,
    gated_v,
    ggate_v,
    fb_acc,
    fa_acc,
    r1s,
    r1r,
    rp,
    r2s,
    r2r,
    tr,
    pr,
    ag1,
    ag2,
    ld_sem,
    snd,
    rcv,
):
    me = lax.axis_index("tm")
    te = lax.axis_index("tensor")
    core = me & 1
    my = (me >> 1) & 3
    mx = (me >> 3) & 3
    mz = me >> 5
    chip = me >> 1

    def each_peer(fn, cores=(0, 1)):
        for dz, dc in ((0, 1), (1, 0), (1, 1)):
            if dc in cores:
                fn((((mz ^ dz) * 4 + mx) * 4 + my) * 2 + (core ^ dc))

        @pl.loop(1, 16)
        def _(p):
            q = (p * 5) & 15
            x = (mx + (q >> 2)) & 3
            y = (my + q) & 3
            for dz in (0, 1):
                for dc in cores:
                    fn((((mz ^ dz) * 4 + x) * 4 + y) * 2 + (core ^ dc))

    loads = [
        pltpu.make_async_copy(cot_h, cot_v, ld_sem.at[0]),
        pltpu.make_async_copy(in_h, in_v, ld_sem.at[1]),
        pltpu.make_async_copy(ker_h, ker_v, ld_sem.at[2]),
    ]
    for cp in loads:
        cp.start()

    barrier = pltpu.get_barrier_semaphore()

    each_peer(
        lambda d: pl.semaphore_signal(barrier, inc=1, device_id=(d, te), device_id_type=MESH)
    )

    for q in range(1, TE):
        pl.semaphore_signal(
            barrier, inc=1, device_id=(me, lax.rem(te + q, TE)), device_id_type=MESH
        )

    def copy_to(src, dst, ph, device):
        return pltpu.make_async_remote_copy(
            src_ref=src,
            dst_ref=dst,
            send_sem=snd.at[ph],
            recv_sem=rcv.at[ph],
            device_id=device,
            device_id_type=MESH,
        )

    def send_all(slot_of, dst, ph):
        each_peer(lambda d: copy_to(slot_of(d), dst.at[me], ph, (d, te)).start())

    def wait_slots(ref, sem, slots=TM - 1):
        part = ref.at[pl.ds(0, slots)]
        pltpu.make_async_copy(part, part, sem).wait()

    loads[0].wait()
    loads[1].wait()

    @pl.loop(0, N2 // CR)
    def _(c):
        for n in range(NB):
            gate = nn(four(in_v, c, n), w_gate[n])
            gg = nt(four(cot_v, c, n), w_out[n])
            put_four(gate_v, c, n, gate)
            put_four(gg_v, c, n, gg)
            so_g[pl.ds(c * DC, DC), :, lanes(n)] = (
                by_dest(gate * gg).astype(BF16).reshape(DC, LOC * KD, 128)
            )

    pl.semaphore_wait(barrier, TM - 1 + TE - 1)
    send_all(lambda d: so_g.at[d], rc_g, 0)

    for s in range(4):
        a_t[:, lanes(s)] = fa[lanes(s), :].T

    @pl.loop(0, LOC)
    def _(i):
        rows = pl.ds(pl.multiple_of(i * N2, N2), N2)
        for n in range(NB):
            mx_v[rows, lanes(n)] = nn(in_v[rows, lanes(n)], w_in[n]).astype(BF16)
        first_v[rows, :] = nn(a_t[...], mx_v[rows, :])

    loads[2].wait()

    @pl.loop(0, N2 // CR)
    def _(c):
        for n in range(NB):
            tw = four(first_v, c, n) * four(ker_v, c, n).astype(F32)
            so_f[pl.ds(c * DC, DC), :, lanes(n)] = (
                by_dest(tw).astype(BF16).reshape(DC, LOC * KD, 128)
            )

    send_all(lambda d: so_f.at[d], rc_f, 1)
    rc_g[me] = so_g[me]
    rc_f[me] = so_f[me]

    b_t[...] = fb[...].T

    @pl.loop(0, ROWS // 256)
    def _(c):
        rows = pl.ds(pl.multiple_of(c * 256, 256), 256)
        for n in range(NB):
            in_t[n, :, rows] = in_v[rows, lanes(n)].T
            cot_t[n, :, rows] = cot_v[rows, lanes(n)].T

    def columns(rc, x):
        @pl.loop(0, 8)
        def _(c):
            rows = pl.ds(pl.multiple_of(c * 256, 256), 256)
            for n in range(NB):
                xs[n, rows, :] = rc[pl.ds(c * 8, 8), :, lanes(n)].reshape(256, 128).astype(F32)

        for k in range(KD):
            for n in range(NB):
                x[k, :, lanes(n)] = xs[n, pl.ds(k, N1, stride=KD), :].astype(BF16)

    def product(lhs, x, sr):
        for k in range(KD):
            y = nn(lhs[...], x[k])
            for n in range(NB):
                xs[n, pl.ds(k, N1, stride=KD), :] = y[:, lanes(n)]

        @pl.loop(0, 8)
        def _(c):
            rows = pl.ds(pl.multiple_of(c * 256, 256), 256)
            for n in range(NB):
                sr[pl.ds(c * 8, 8), :, lanes(n)] = (
                    xs[n, rows, :].astype(BF16).reshape(8, LOC * KD, 128)
                )

    wait_slots(rc_g, rcv.at[0])
    columns(rc_g, x_g)
    product(fb, x_g, sr_g)
    send_all(lambda d: sr_g.at[d], rr_g, 2)
    rr_g[me] = sr_g[me]

    wait_slots(rc_f, rcv.at[1])
    columns(rc_f, x_f)
    product(b_t, x_f, sr_f)
    send_all(lambda d: sr_f.at[d], rr_f, 3)
    rr_f[me] = sr_f[me]

    fb_acc[...] = nt(x_f[0], x_g[0])

    @pl.loop(1, KD)
    def _(k):
        fb_acc[...] += nt(x_f[k], x_g[k])

    for h in range(2):
        r1s[:, h, :, 512:640] = fb_acc[:, lanes(h)].reshape(TM // 2, 8, 128)

    wait_slots(rr_g, rcv.at[2])

    @pl.loop(0, N2 // CR)
    def _(c):
        for n in range(NB):
            gt = by_block(
                rr_g[pl.ds(c * DC, DC), :, lanes(n)].reshape(LOC * CR, 128).astype(F32)
            )
            gf = (gt * four(ker_v, c, n).astype(F32)).astype(BF16)
            gk = (gt * four(first_v, c, n)).astype(BF16)
            put_four(gf_v, c, n, gf)
            put_four(gker_v, c, n, gk)

    fa_acc[...] = jnp.zeros_like(fa_acc)

    @pl.loop(0, LOC)
    def _(i):
        rows = pl.ds(pl.multiple_of(i * N2, N2), N2)
        gm_v[rows, :] = nn(fa[...], gf_v[rows, :]).astype(BF16)
        fa_acc[...] += nt(mx_v[rows, :], gf_v[rows, :])

    r1s[:, :, :, 0:512] = fa_acc[...].reshape(TM // 2, 2, 8, 512)
    for n in range(NB):
        r1s[n * 8 : (n + 1) * 8, :, :, 640:768] = nn(in_t[n], gm_v[:, lanes(n)]).reshape(
            8, 2, 8, 128
        )
    r1s[24:32, :, :, 640:768] = jnp.zeros((8, 2, 8, 128), F32)
    half = copy_to(r1s.at[:, 1 - core], rp, 10, (me ^ 1, te))
    half.start()
    half.wait_recv()

    @pl.loop(0, TM // 2)
    def _(g):
        rp[g] += r1s[g, core]

    each_peer(
        lambda d: copy_to(rp.at[d >> 1], r1r.at[chip], 4, (d, te)).start(), cores=(0,)
    )
    r1r[chip] = rp[chip]

    wait_slots(rr_f, rcv.at[3])

    @pl.loop(0, N2 // CR)
    def _(c):
        for n in range(NB):
            sec = by_block(
                rr_f[pl.ds(c * DC, DC), :, lanes(n)].reshape(LOC * CR, 128).astype(F32)
            )
            put_four(gated_v, c, n, (sec * four(gate_v, c, n)).astype(BF16))
            put_four(ggate_v, c, n, (sec * four(gg_v, c, n)).astype(BF16))

    for n in range(NB):
        r2s[n * 16 : (n + 1) * 16, 0] = nn(in_t[n], ggate_v[:, lanes(n)]).reshape(16, 8, 128)
        r2s[n * 16 : (n + 1) * 16, 1] = nn(cot_t[n], gated_v[:, lanes(n)]).T.reshape(16, 8, 128)

    def send_r2(d):
        @pl.when(d < OWN)
        def _():
            copy_to(r2s.at[d], r2r.at[me], 7, (d, te)).start()

    each_peer(send_r2)

    @pl.when(me < OWN)
    def _():
        r2r[me] = r2s[me]

    @pl.loop(0, ROWS // 256)
    def _(c):
        rows = pl.ds(pl.multiple_of(c * 256, 256), 256)
        for n in range(NB):
            out_v[rows, lanes(n)] = nn(gated_v[rows, lanes(n)], w_out[n]).astype(BF16)
            gin_v[rows, lanes(n)] = (
                nt(gm_v[rows, lanes(n)], w_in[n]) + nt(ggate_v[rows, lanes(n)], w_gate[n])
            ).astype(BF16)

    def four_slots(q):
        return (r1r[q * 4] + r1r[q * 4 + 1]) + (r1r[q * 4 + 2] + r1r[q * 4 + 3])

    token_scale = 1.0 / math.sqrt(N1 * N2)
    wait_slots(r1r, rcv.at[4], TM // 2 - 1)
    sum1 = lax.fori_loop(0, TM // 8, lambda q, acc: acc + four_slots(q), jnp.zeros((8, 768), F32))
    tr[te] = sum1[:, 0:640]
    for q in range(1, TE):
        copy_to(tr.at[te], tr.at[te], 5, (me, lax.rem(te + q, TE))).start()

    @pl.when(me < OWN)
    def _():
        ag1[me] = sum1[:, 640:768] * token_scale
        send_all(lambda d: ag1.at[me], ag1, 8)
        wait_slots(r2r, rcv.at[7])
        ag2[me] = jnp.sum(r2r[...], axis=0) * token_scale
        send_all(lambda d: ag2.at[me], ag2, 9)

    wait_slots(tr, rcv.at[5], TE - 1)
    total = tr[0] + tr[1] + tr[2] + tr[3]
    gfa[...] = total[:, 0:512] * (1.0 / math.sqrt(N1 * D))
    pr[core] = total[:, 512:640] * (1.0 / math.sqrt(N2 * D))
    pair = copy_to(pr.at[core], pr.at[core], 6, (me + 1 - 2 * core, te))
    pair.start()
    pair.wait()
    for h in range(2):
        gfb[:, lanes(h)] = jnp.where(core == 0, pr[h, 0:4, :], pr[h, 4:8, :])

    def others(fn):
        @pl.when(me < OWN)
        def _():
            fn(OWN - 1)

        @pl.when(me >= OWN)
        def _():
            fn(OWN)

    others(lambda k: wait_slots(ag1, rcv.at[8], k))
    gw_in[...] = ag1[...]
    others(lambda k: wait_slots(ag2, rcv.at[9], k))
    gw_gate[...] = ag2[:, 0]
    gw_out[...] = ag2[:, 1]

    wait_slots(rc_g, snd.at[0])
    wait_slots(rc_f, snd.at[1])
    wait_slots(rr_g, snd.at[2])
    wait_slots(rr_f, snd.at[3])
    wait_slots(r1r, snd.at[4], TM // 2 - 1)
    wait_slots(tr, snd.at[5], TE - 1)
    others(lambda k: wait_slots(r2r, snd.at[7], k))

    @pl.when(me < OWN)
    def _():
        for part in (ag1.at[pl.ds(0, 48)], ag1.at[pl.ds(0, 15)]):
            pltpu.make_async_copy(part, part, snd.at[8]).wait()
        wait_slots(r2r, snd.at[9])

    half.wait_send()


def finish_body(*refs):
    srcs, dsts, sem = refs[:8], refs[8:16], refs[16]
    stores = []
    for src, dst in zip(srcs, dsts, strict=True):
        cuts = 4 if src.shape[0] == ROWS else 1
        step = src.shape[0] // cuts
        for j in range(cuts):
            rows = pl.ds(j * step, step)
            stores.append(pltpu.make_async_copy(src.at[rows], dst.at[rows], sem.at[len(stores)]))
    for cp in stores:
        cp.start()
    for cp in stores:
        cp.wait()


def body(inputs, kernel, w_in, w_gate, w_out, factor_a, factor_b, cotangent):
    any_spec = pl.BlockSpec(memory_space=pl.ANY)
    vm = pl.BlockSpec(memory_space=pltpu.VMEM)
    wide = pltpu.VMEM((ROWS, CH), F32)
    act = pltpu.VMEM((ROWS, CH), BF16)
    turned = pltpu.VMEM((NB, 128, ROWS), BF16)
    slots = pltpu.VMEM((TM, LOC * KD, CH), BF16)
    cols = pltpu.VMEM((KD, N1, CH), BF16)
    tile = pltpu.VMEM((OWN, 8, 128), F32)
    outs = pl.pallas_call(
        kernel_body,
        name="monarch",
        out_shape=(
            act,
            act,
            act,
            tile,
            tile,
            tile,
            pltpu.VMEM((8, N2), F32),
            pltpu.VMEM((4, N1), F32),
        ),
        in_specs=[any_spec, any_spec, vm, vm, vm, vm, vm, any_spec],
        out_specs=(vm,) * 8,
        scratch_shapes=[
            act,
            act,
            act,
            turned,
            turned,
            pltpu.VMEM((N2, N2), BF16),
            pltpu.VMEM((N1, N1), BF16),
            wide,
            wide,
            wide,
            act,
            slots,
            slots,
            slots,
            slots,
            pltpu.VMEM((NB, ROWS, 128), F32),
            cols,
            cols,
            slots,
            slots,
            slots,
            slots,
            act,
            act,
            act,
            act,
            pltpu.VMEM((N1, N1), F32),
            pltpu.VMEM((N2, N2), F32),
            pltpu.VMEM((TM // 2, 2, 8, 768), F32),
            pltpu.VMEM((TM // 2, 8, 768), F32),
            pltpu.VMEM((TM // 2, 8, 768), F32),
            pltpu.VMEM((OWN, 2, 8, 128), F32),
            pltpu.VMEM((TM, 2, 8, 128), F32),
            pltpu.VMEM((TE, 8, 640), F32),
            pltpu.VMEM((2, 8, 128), F32),
            pltpu.VMEM((OWN, 8, 128), F32),
            pltpu.VMEM((OWN, 2, 8, 128), F32),
            pltpu.SemaphoreType.DMA((3,)),
            pltpu.SemaphoreType.DMA((11,)),
            pltpu.SemaphoreType.DMA((11,)),
        ],
        compiler_params=pltpu.CompilerParams(
            collective_id=0, has_side_effects=True, vmem_limit_bytes=57 << 20
        ),
    )(inputs, kernel, w_in, w_gate, w_out, factor_a, factor_b, cotangent)
    outs = pl.pallas_call(
        finish_body,
        name="finish",
        out_shape=tuple(jax.ShapeDtypeStruct(o.shape, o.dtype) for o in outs),
        in_specs=[vm] * len(outs),
        out_specs=(any_spec,) * len(outs),
        scratch_shapes=[pltpu.SemaphoreType.DMA((17,))],
        compiler_params=pltpu.CompilerParams(vmem_limit_bytes=8 << 20),
    )(*outs)
    out, gin, gker, gwi, gwg, gwo, gfa, gfb = outs
    shape = (NB, 128, 128)
    return (
        out,
        gin,
        gker,
        gwi.reshape(shape),
        gwg.reshape(shape),
        gwo.reshape(shape),
        gfa,
        gfb,
    )


def solution(mesh):
    return jax.shard_map(
        body,
        mesh=mesh,
        in_specs=(
            P("tm", "tensor"),
            P("tm", "tensor"),
            P("tensor", None, None),
            P("tensor", None, None),
            P("tensor", None, None),
            P(),
            P(),
            P("tm", "tensor"),
        ),
        out_specs=(
            P("tm", "tensor"),
            P("tm", "tensor"),
            P("tm", "tensor"),
            P("tensor", None, None),
            P("tensor", None, None),
            P("tensor", None, None),
            P("tm", None),
            P("tm", None),
        ),
        check_vma=False,
    )
```

```python
import math

import jax
import jax.numpy as jnp
from jax import lax
from jax.experimental import pallas as pl
from jax.experimental.pallas import tpu as pltpu
from jax.sharding import PartitionSpec as P

D = 1536
N1 = 256
N2 = 512
MESH = pl.DeviceIdType.MESH
F32 = jnp.float32
BF16 = jnp.bfloat16
TM = 64
TE = 4
ROWS = 2048
CH = 384
LOC = 4
KD = 8
NB = 3
OWN = 48
DC = 8
CR = DC * KD


def lanes(n):
    return slice(n * 128, (n + 1) * 128)


def nt(a, b):
    return lax.dot_general(a, b, (((1,), (1,)), ((), ())), preferred_element_type=F32)


def nn(a, b):
    return jnp.dot(a, b, preferred_element_type=F32)


def four(ref, c, n):
    return jnp.concatenate(
        [ref[pl.ds(i * N2 + c * CR, CR), lanes(n)] for i in range(LOC)], axis=0
    )


def put_four(ref, c, n, val):
    for i in range(LOC):
        ref[pl.ds(i * N2 + c * CR, CR), lanes(n)] = val[i * CR : (i + 1) * CR]


def by_dest(val):
    return jnp.concatenate(
        [
            val[i * CR + d * KD : i * CR + (d + 1) * KD]
            for d in range(DC)
            for i in range(LOC)
        ],
        axis=0,
    )


def by_block(val):
    return jnp.concatenate(
        [
            val[(d * LOC + i) * KD : (d * LOC + i + 1) * KD]
            for i in range(LOC)
            for d in range(DC)
        ],
        axis=0,
    )


def kernel_body(
    in_h,
    ker_h,
    wi_h,
    wg_h,
    wo_h,
    fa_h,
    fb_h,
    cot_h,
    out_v,
    gin_v,
    gker_v,
    gw_in,
    gw_gate,
    gw_out,
    gfa,
    gfb,
    in_v,
    ker_v,
    cot_v,
    w_in,
    w_gate,
    w_out,
    fa,
    fb,
    in_t,
    cot_t,
    a_t,
    b_t,
    gate_v,
    gg_v,
    first_v,
    mx_v,
    so_g,
    so_f,
    rc_g,
    rc_f,
    xs,
    x_g,
    x_f,
    sr_g,
    sr_f,
    rr_g,
    rr_f,
    gf_v,
    gm_v,
    gated_v,
    ggate_v,
    fb_acc,
    fa_acc,
    r1s,
    r1r,
    r1b,
    rp,
    r2s,
    r2r,
    tr,
    pr,
    ag1,
    ag2,
    ld_sem,
    snd,
    rcv,
):
    me = lax.axis_index("tm")
    te = lax.axis_index("tensor")
    core = me & 1
    my = (me >> 1) & 3
    mx = (me >> 3) & 3
    mz = me >> 5
    chip = me >> 1

    def each_peer(fn, cores=(0, 1)):
        for dz, dc in ((0, 1), (1, 0), (1, 1)):
            if dc in cores:
                fn((((mz ^ dz) * 4 + mx) * 4 + my) * 2 + (core ^ dc))

        @pl.loop(1, 16)
        def _(p):
            q = (p * 5) & 15
            x = (mx + (q >> 2)) & 3
            y = (my + q) & 3
            for dz in (0, 1):
                for dc in cores:
                    fn((((mz ^ dz) * 4 + x) * 4 + y) * 2 + (core ^ dc))

    loads = [
        pltpu.make_async_copy(src, dst, ld_sem.at[j])
        for j, (src, dst) in enumerate(
            (
                (wg_h, w_gate),
                (wo_h, w_out),
                (cot_h, cot_v),
                (in_h, in_v),
                (wi_h, w_in),
                (fa_h, fa),
                (ker_h, ker_v),
                (fb_h, fb),
            )
        )
    ]
    for cp in loads:
        cp.start()

    barrier = pltpu.get_barrier_semaphore()

    each_peer(
        lambda d: pl.semaphore_signal(barrier, inc=1, device_id=(d, te), device_id_type=MESH)
    )

    for q in range(1, TE):
        pl.semaphore_signal(
            barrier, inc=1, device_id=(me, lax.rem(te + q, TE)), device_id_type=MESH
        )

    def copy_to(src, dst, ph, device):
        return pltpu.make_async_remote_copy(
            src_ref=src,
            dst_ref=dst,
            send_sem=snd.at[ph],
            recv_sem=rcv.at[ph],
            device_id=device,
            device_id_type=MESH,
        )

    def send_all(slot_of, dst, ph):
        each_peer(lambda d: copy_to(slot_of(d), dst.at[me], ph, (d, te)).start())

    def wait_slots(ref, sem, slots=TM - 1):
        part = ref.at[pl.ds(0, slots)]
        pltpu.make_async_copy(part, part, sem).wait()

    for cp in loads[:4]:
        cp.wait()

    @pl.loop(0, N2 // CR)
    def _(c):
        for n in range(NB):
            gate = nn(four(in_v, c, n), w_gate[n])
            gg = nt(four(cot_v, c, n), w_out[n])
            put_four(gate_v, c, n, gate)
            put_four(gg_v, c, n, gg)
            so_g[pl.ds(c * DC, DC), :, lanes(n)] = (
                by_dest(gate * gg).astype(BF16).reshape(DC, LOC * KD, 128)
            )

    pl.semaphore_wait(barrier, TM - 1 + TE - 1)
    send_all(lambda d: so_g.at[d], rc_g, 0)

    loads[4].wait()
    loads[5].wait()
    for s in range(4):
        a_t[:, lanes(s)] = fa[lanes(s), :].T

    @pl.loop(0, LOC)
    def _(i):
        rows = pl.ds(pl.multiple_of(i * N2, N2), N2)
        for n in range(NB):
            mx_v[rows, lanes(n)] = nn(in_v[rows, lanes(n)], w_in[n]).astype(BF16)
        first_v[rows, :] = nn(a_t[...], mx_v[rows, :])

    loads[6].wait()

    @pl.loop(0, N2 // CR)
    def _(c):
        for n in range(NB):
            tw = four(first_v, c, n) * four(ker_v, c, n).astype(F32)
            so_f[pl.ds(c * DC, DC), :, lanes(n)] = (
                by_dest(tw).astype(BF16).reshape(DC, LOC * KD, 128)
            )

    send_all(lambda d: so_f.at[d], rc_f, 1)
    rc_g[me] = so_g[me]
    rc_f[me] = so_f[me]

    loads[7].wait()
    b_t[...] = fb[...].T

    @pl.loop(0, ROWS // 256)
    def _(c):
        rows = pl.ds(pl.multiple_of(c * 256, 256), 256)
        for n in range(NB):
            in_t[n, :, rows] = in_v[rows, lanes(n)].T
            cot_t[n, :, rows] = cot_v[rows, lanes(n)].T

    def columns(rc, x):
        @pl.loop(0, 8)
        def _(c):
            rows = pl.ds(pl.multiple_of(c * 256, 256), 256)
            for n in range(NB):
                xs[n, rows, :] = rc[pl.ds(c * 8, 8), :, lanes(n)].reshape(256, 128).astype(F32)

        for k in range(KD):
            for n in range(NB):
                x[k, :, lanes(n)] = xs[n, pl.ds(k, N1, stride=KD), :].astype(BF16)

    def product(lhs, x, slab):
        for k in range(KD):
            y = nn(lhs[...], x[k])
            for n in range(NB):
                xs[n, pl.ds(k, N1, stride=KD), :] = y[:, lanes(n)]

        @pl.loop(0, 8)
        def _(c):
            rows = pl.ds(pl.multiple_of(c * 256, 256), 256)
            for n in range(NB):
                slab(c, n)[...] = xs[n, rows, :].astype(BF16).reshape(8, LOC * KD, 128)

    wait_slots(rc_g, rcv.at[0])
    columns(rc_g, x_g)
    product(fb, x_g, lambda c, n: sr_g.at[pl.ds(c * 8, 8), :, lanes(n)])
    send_all(lambda d: sr_g.at[d], rr_g, 2)
    rr_g[me] = sr_g[me]

    wait_slots(rc_f, rcv.at[1])
    columns(rc_f, x_f)
    product(b_t, x_f, lambda c, n: sr_f.at[n, pl.ds(c * 8, 8)])
    for n in range(NB):
        send_all(lambda d, n=n: sr_f.at[n, d], rr_f.at[n], 3 + n)
    for n in range(NB):
        rr_f[n, me] = sr_f[n, me]

    fb_acc[...] = nt(x_f[0], x_g[0])

    @pl.loop(1, KD)
    def _(k):
        fb_acc[...] += nt(x_f[k], x_g[k])

    for h in range(2):
        r1s[:, h, :, 512:640] = fb_acc[:, lanes(h)].reshape(TM // 2, 8, 128)

    wait_slots(rr_g, rcv.at[2])

    @pl.loop(0, N2 // CR)
    def _(c):
        for n in range(NB):
            gt = by_block(
                rr_g[pl.ds(c * DC, DC), :, lanes(n)].reshape(LOC * CR, 128).astype(F32)
            )
            gf = (gt * four(ker_v, c, n).astype(F32)).astype(BF16)
            gk = (gt * four(first_v, c, n)).astype(BF16)
            put_four(gf_v, c, n, gf)
            put_four(gker_v, c, n, gk)

    fa_acc[...] = jnp.zeros_like(fa_acc)

    @pl.loop(0, LOC)
    def _(i):
        rows = pl.ds(pl.multiple_of(i * N2, N2), N2)
        gm_v[rows, :] = nn(fa[...], gf_v[rows, :]).astype(BF16)
        fa_acc[...] += nt(mx_v[rows, :], gf_v[rows, :])

    r1s[:, :, :, 0:512] = fa_acc[...].reshape(TM // 2, 2, 8, 512)
    for n in range(NB):
        r1s[n * 8 : (n + 1) * 8, :, :, 640:768] = nn(in_t[n], gm_v[:, lanes(n)]).reshape(
            8, 2, 8, 128
        )
    r1s[24:32, :, :, 640:768] = jnp.zeros((8, 2, 8, 128), F32)
    half = copy_to(r1s.at[:, 1 - core], rp, 9, (me ^ 1, te))
    half.start()

    def forward_tail(n):
        wait_slots(rr_f.at[n], rcv.at[3 + n])

        @pl.loop(0, N2 // CR)
        def _(c):
            sec = by_block(
                rr_f[n, pl.ds(c * DC, DC)].reshape(LOC * CR, 128).astype(F32)
            )
            put_four(gated_v, c, n, (sec * four(gate_v, c, n)).astype(BF16))
            put_four(ggate_v, c, n, (sec * four(gg_v, c, n)).astype(BF16))

        r2s[n, 0:16] = nn(in_t[n], ggate_v[:, lanes(n)]).reshape(16, 8, 128)
        r2s[n, 16:32] = nn(cot_t[n], gated_v[:, lanes(n)]).T.reshape(16, 8, 128)
        own = n % 2

        def send(d):
            @pl.when((d & 1) == own)
            def _():
                copy_to(r2s.at[n, d >> 1], r2r.at[n, me], 11 + n, (d, te)).start()

        each_peer(send)

        @pl.when(core == own)
        def _():
            r2r[n, me] = r2s[n, chip]

    forward_tail(0)
    half.wait_recv()

    @pl.loop(0, TM // 2)
    def _(g):
        both = rp[g] + r1s[g, core]
        r1b[g] = jnp.concatenate([both[:, 0:CH], both[:, CH:]], axis=0).astype(BF16)

    each_peer(
        lambda d: copy_to(r1b.at[d >> 1], r1r.at[chip], 6, (d, te)).start(), cores=(0,)
    )
    r1r[chip] = r1b[chip]
    forward_tail(1)
    forward_tail(2)

    @pl.loop(0, ROWS // 256)
    def _(c):
        rows = pl.ds(pl.multiple_of(c * 256, 256), 256)
        for n in range(NB):
            out_v[rows, lanes(n)] = nn(gated_v[rows, lanes(n)], w_out[n]).astype(BF16)
            gin_v[rows, lanes(n)] = (
                nt(gm_v[rows, lanes(n)], w_in[n]) + nt(ggate_v[rows, lanes(n)], w_gate[n])
            ).astype(BF16)

    def four_slots(q):
        a, b, c, d = (r1r[q * 4 + j].astype(F32) for j in range(4))
        return (a + b) + (c + d)

    token_scale = 1.0 / math.sqrt(N1 * N2)
    wait_slots(r1r, rcv.at[6], TM // 2 - 1)
    sum1 = lax.fori_loop(0, TM // 8, lambda q, acc: acc + four_slots(q), jnp.zeros((16, CH), F32))
    tr[te, :, 0:CH] = sum1[0:8]
    tr[te, :, CH:640] = sum1[8:16, 0:256]
    for q in range(1, TE):
        copy_to(tr.at[te], tr.at[te], 7, (me, lax.rem(te + q, TE))).start()

    def to_chips(piece, ph):
        each_peer(lambda d: copy_to(piece, piece, ph, (d, te)).start(), cores=(0,))

    @pl.when(me < OWN)
    def _():
        ag1[chip, core] = sum1[8:16, 256:CH] * token_scale
        to_chips(ag1.at[chip, core], 10)

    for n in range(NB):

        @pl.when(core == n % 2)
        def _(n=n):
            wait_slots(r2r.at[n], rcv.at[11 + n])
            ag2[n, chip] = jnp.sum(r2r[n], axis=0) * token_scale
            to_chips(ag2.at[n, chip], 14 + n)

    wait_slots(tr, rcv.at[7], TE - 1)
    total = tr[0] + tr[1] + tr[2] + tr[3]
    gfa[...] = total[:, 0:512] * (1.0 / math.sqrt(N1 * D))
    pr[core] = total[:, 512:640] * (1.0 / math.sqrt(N2 * D))
    pair = copy_to(pr.at[core], pr.at[core], 8, (me ^ 1, te))
    pair.start()
    pair.wait()
    for h in range(2):
        gfb[:, lanes(h)] = jnp.where(core == 0, pr[h, 0:4, :], pr[h, 4:8, :])

    def either(cond, then, other):
        @pl.when(cond)
        def _():
            then()

        @pl.when(jnp.logical_not(cond))
        def _():
            other()

    other = (me ^ 1, te)
    either(
        me < OWN,
        lambda: wait_slots(ag2.at[0], rcv.at[10], OWN // 2 - 1),
        lambda: wait_slots(ag2.at[0], rcv.at[10], OWN // 2),
    )
    pass1 = copy_to(ag1.at[:, core], ag1.at[:, core], 17, other)
    pass1.start()
    for n in range(NB):

        @pl.when(core == n % 2)
        def _(n=n):
            wait_slots(ag2.at[n], rcv.at[14 + n], TM // 2 - 1)
            copy_to(ag2.at[n], ag2.at[n], 18 + n, other).start()

    pass1.wait_recv()
    gw_in[...] = ag1[...].reshape(OWN, 8, 128)
    for n in range(NB):

        @pl.when(core != n % 2)
        def _(n=n):
            wait_slots(ag2.at[n], rcv.at[18 + n], TM // 2)

        gw_gate[n * 16 : (n + 1) * 16] = ag2[n, 0:16]
        gw_out[n * 16 : (n + 1) * 16] = ag2[n, 16:32]

    wait_slots(rc_g, snd.at[0])
    wait_slots(rc_f, snd.at[1])
    wait_slots(rr_g, snd.at[2])
    for n in range(NB):
        wait_slots(rr_f.at[n], snd.at[3 + n])
        either(
            core == n % 2,
            lambda: wait_slots(r2r.at[n], snd.at[11 + n], TM // 2 - 1),
            lambda: wait_slots(r2r.at[n], snd.at[11 + n], TM // 2),
        )

        @pl.when(core == n % 2)
        def _(n=n):
            wait_slots(ag2.at[n], snd.at[14 + n], TM // 2 - 1)
            wait_slots(ag2.at[n], snd.at[18 + n], TM // 2)

    wait_slots(r1r, snd.at[6], TM // 2 - 1)
    wait_slots(tr, snd.at[7], TE - 1)
    half.wait_send()
    pass1.wait_send()

    @pl.when(me < OWN)
    def _():
        wait_slots(ag2.at[0], snd.at[10], TM // 2 - 1)


def finish_body(*refs):
    srcs, dsts, sem = refs[:8], refs[8:16], refs[16]
    stores = []
    for src, dst in zip(srcs, dsts, strict=True):
        cuts = 4 if src.shape[0] == ROWS else 1
        step = src.shape[0] // cuts
        for j in range(cuts):
            rows = pl.ds(j * step, step)
            stores.append(pltpu.make_async_copy(src.at[rows], dst.at[rows], sem.at[len(stores)]))
    for cp in stores:
        cp.start()
    for cp in stores:
        cp.wait()


def body(inputs, kernel, w_in, w_gate, w_out, factor_a, factor_b, cotangent):
    any_spec = pl.BlockSpec(memory_space=pl.ANY)
    vm = pl.BlockSpec(memory_space=pltpu.VMEM)
    wide = pltpu.VMEM((ROWS, CH), F32)
    act = pltpu.VMEM((ROWS, CH), BF16)
    turned = pltpu.VMEM((NB, 128, ROWS), BF16)
    slots = pltpu.VMEM((TM, LOC * KD, CH), BF16)
    mixer = pltpu.VMEM((NB, 128, 128), BF16)
    slots_n = pltpu.VMEM((NB, TM, LOC * KD, 128), BF16)
    cols = pltpu.VMEM((KD, N1, CH), BF16)
    tile = pltpu.VMEM((OWN, 8, 128), F32)
    outs = pl.pallas_call(
        kernel_body,
        name="monarch",
        out_shape=(
            act,
            act,
            act,
            tile,
            tile,
            tile,
            pltpu.VMEM((8, N2), F32),
            pltpu.VMEM((4, N1), F32),
        ),
        in_specs=[any_spec] * 8,
        out_specs=(vm,) * 8,
        scratch_shapes=[
            act,
            act,
            act,
            mixer,
            mixer,
            mixer,
            pltpu.VMEM((N2, N2), BF16),
            pltpu.VMEM((N1, N1), BF16),
            turned,
            turned,
            pltpu.VMEM((N2, N2), BF16),
            pltpu.VMEM((N1, N1), BF16),
            wide,
            wide,
            wide,
            act,
            slots,
            slots,
            slots,
            slots,
            pltpu.VMEM((NB, ROWS, 128), F32),
            cols,
            cols,
            slots,
            slots_n,
            slots,
            slots_n,
            act,
            act,
            act,
            act,
            pltpu.VMEM((N1, N1), F32),
            pltpu.VMEM((N2, N2), F32),
            pltpu.VMEM((TM // 2, 2, 8, 768), F32),
            pltpu.VMEM((TM // 2, 16, CH), BF16),
            pltpu.VMEM((TM // 2, 16, CH), BF16),
            pltpu.VMEM((TM // 2, 8, 768), F32),
            pltpu.VMEM((NB, TM // 2, 8, 128), F32),
            pltpu.VMEM((NB, TM, 8, 128), F32),
            pltpu.VMEM((TE, 8, 640), F32),
            pltpu.VMEM((2, 8, 128), F32),
            pltpu.VMEM((OWN // 2, 2, 8, 128), F32),
            pltpu.VMEM((NB, TM // 2, 8, 128), F32),
            pltpu.SemaphoreType.DMA((8,)),
            pltpu.SemaphoreType.DMA((21,)),
            pltpu.SemaphoreType.DMA((21,)),
        ],
        compiler_params=pltpu.CompilerParams(
            collective_id=0, has_side_effects=True, vmem_limit_bytes=57 << 20
        ),
    )(inputs, kernel, w_in, w_gate, w_out, factor_a, factor_b, cotangent)
    outs = pl.pallas_call(
        finish_body,
        name="finish",
        out_shape=tuple(jax.ShapeDtypeStruct(o.shape, o.dtype) for o in outs),
        in_specs=[vm] * len(outs),
        out_specs=(any_spec,) * len(outs),
        scratch_shapes=[pltpu.SemaphoreType.DMA((17,))],
        compiler_params=pltpu.CompilerParams(vmem_limit_bytes=8 << 20),
    )(*outs)
    out, gin, gker, gwi, gwg, gwo, gfa, gfb = outs
    shape = (NB, 128, 128)
    return (
        out,
        gin,
        gker,
        gwi.reshape(shape),
        gwg.reshape(shape),
        gwo.reshape(shape),
        gfa,
        gfb,
    )


def solution(mesh):
    return jax.shard_map(
        body,
        mesh=mesh,
        in_specs=(
            P("tm", "tensor"),
            P("tm", "tensor"),
            P("tensor", None, None),
            P("tensor", None, None),
            P("tensor", None, None),
            P(),
            P(),
            P("tm", "tensor"),
        ),
        out_specs=(
            P("tm", "tensor"),
            P("tm", "tensor"),
            P("tm", "tensor"),
            P("tensor", None, None),
            P("tensor", None, None),
            P("tensor", None, None),
            P("tm", None),
            P("tm", None),
        ),
        check_vma=False,
    )
```

```python
import math

import jax
import jax.numpy as jnp
from jax import lax
from jax.experimental import pallas as pl
from jax.experimental.pallas import tpu as pltpu
from jax.sharding import PartitionSpec as P

D = 1536
N1 = 256
N2 = 512
MESH = pl.DeviceIdType.MESH
F32 = jnp.float32
BF16 = jnp.bfloat16
TM = 64
TE = 4
ROWS = 2048
CH = 384
LOC = 4
KD = 8
NB = 3
OWN = 48
DC = 8
CR = DC * KD


def lanes(n):
    return slice(n * 128, (n + 1) * 128)


def nt(a, b):
    return lax.dot_general(a, b, (((1,), (1,)), ((), ())), preferred_element_type=F32)


def nn(a, b):
    return jnp.dot(a, b, preferred_element_type=F32)


def four(ref, c, n):
    return jnp.concatenate(
        [ref[pl.ds(i * N2 + c * CR, CR), lanes(n)] for i in range(LOC)], axis=0
    )


def put_four(ref, c, n, val):
    for i in range(LOC):
        ref[pl.ds(i * N2 + c * CR, CR), lanes(n)] = val[i * CR : (i + 1) * CR]


def by_dest(val):
    return jnp.concatenate(
        [
            val[i * CR + d * KD : i * CR + (d + 1) * KD]
            for d in range(DC)
            for i in range(LOC)
        ],
        axis=0,
    )


def by_block(val):
    return jnp.concatenate(
        [
            val[(d * LOC + i) * KD : (d * LOC + i + 1) * KD]
            for i in range(LOC)
            for d in range(DC)
        ],
        axis=0,
    )


def kernel_body(
    in_h,
    ker_h,
    wi_h,
    wg_h,
    wo_h,
    fa_h,
    fb_h,
    cot_h,
    out_v,
    gin_v,
    gker_v,
    gw_in,
    gw_gate,
    gw_out,
    gfa,
    gfb,
    in_v,
    ker_v,
    cot_v,
    w_in,
    w_gate,
    w_out,
    fa,
    fb,
    in_t,
    cot_t,
    a_t,
    b_t,
    gate_v,
    gg_v,
    first_v,
    mx_v,
    so_g,
    so_f,
    rc_g,
    rc_f,
    xs,
    x_g,
    x_f,
    sr_g,
    sr_f,
    rr_g,
    rr_f,
    gf_v,
    gm_v,
    gated_v,
    ggate_v,
    fb_acc,
    fa_acc,
    r1s,
    r1r,
    r1b,
    rp,
    r2s,
    r2r,
    tr,
    pr,
    ag1,
    ag2,
    ld_sem,
    snd,
    rcv,
):
    me = lax.axis_index("tm")
    te = lax.axis_index("tensor")
    core = me & 1
    my = (me >> 1) & 3
    mx = (me >> 3) & 3
    mz = me >> 5
    chip = me >> 1

    def each_peer(fn, cores=(0, 1)):
        for dz, dc in ((1, 1), (0, 1), (1, 0), (0, 0)):
            if dc in cores:
                here = dz + dc == 0

                @pl.loop(int(here), 16, unroll=3 if here else 4)
                def _(p, dz=dz, dc=dc):
                    q = (p * 5) & 15
                    x = (mx + (q >> 2)) & 3
                    y = (my + q) & 3
                    fn((((mz ^ dz) * 4 + x) * 4 + y) * 2 + (core ^ dc))

    loads = [
        pltpu.make_async_copy(src, dst, ld_sem.at[j])
        for j, (src, dst) in enumerate(
            (
                (wg_h, w_gate),
                (wo_h, w_out),
                (cot_h, cot_v),
                (in_h, in_v),
                (wi_h, w_in),
                (fa_h, fa),
                (ker_h, ker_v),
                (fb_h, fb),
            )
        )
    ]
    for cp in loads:
        cp.start()

    barrier = pltpu.get_barrier_semaphore()

    each_peer(
        lambda d: pl.semaphore_signal(barrier, inc=1, device_id=(d, te), device_id_type=MESH)
    )

    for q in range(1, TE):
        pl.semaphore_signal(
            barrier, inc=1, device_id=(me, lax.rem(te + q, TE)), device_id_type=MESH
        )

    def copy_to(src, dst, ph, device):
        return pltpu.make_async_remote_copy(
            src_ref=src,
            dst_ref=dst,
            send_sem=snd.at[ph],
            recv_sem=rcv.at[ph],
            device_id=device,
            device_id_type=MESH,
        )

    def send_all(slot_of, dst, ph):
        each_peer(lambda d: copy_to(slot_of(d), dst.at[me], ph, (d, te)).start())

    def wait_slots(ref, sem, slots=TM - 1):
        part = ref.at[pl.ds(0, slots)]
        pltpu.make_async_copy(part, part, sem).wait()

    for cp in loads[:4]:
        cp.wait()

    @pl.loop(0, N2 // CR)
    def _(c):
        for n in range(NB):
            gate = nn(four(in_v, c, n), w_gate[n])
            gg = nt(four(cot_v, c, n), w_out[n])
            put_four(gate_v, c, n, gate)
            put_four(gg_v, c, n, gg)
            so_g[pl.ds(c * DC, DC), :, lanes(n)] = (
                by_dest(gate * gg).astype(BF16).reshape(DC, LOC * KD, 128)
            )

    pl.semaphore_wait(barrier, TM - 1 + TE - 1)
    send_all(lambda d: so_g.at[d], rc_g, 0)

    loads[4].wait()
    loads[5].wait()
    for s in range(4):
        a_t[:, lanes(s)] = fa[lanes(s), :].T

    @pl.loop(0, LOC)
    def _(i):
        rows = pl.ds(pl.multiple_of(i * N2, N2), N2)
        for n in range(NB):
            mx_v[rows, lanes(n)] = nn(in_v[rows, lanes(n)], w_in[n]).astype(BF16)
        first_v[rows, :] = nn(a_t[...], mx_v[rows, :])

    loads[6].wait()

    @pl.loop(0, N2 // CR)
    def _(c):
        for n in range(NB):
            tw = four(first_v, c, n) * four(ker_v, c, n).astype(F32)
            so_f[pl.ds(c * DC, DC), :, lanes(n)] = (
                by_dest(tw).astype(BF16).reshape(DC, LOC * KD, 128)
            )

    send_all(lambda d: so_f.at[d], rc_f, 1)
    rc_g[me] = so_g[me]
    rc_f[me] = so_f[me]

    loads[7].wait()
    b_t[...] = fb[...].T

    @pl.loop(0, ROWS // 256)
    def _(c):
        rows = pl.ds(pl.multiple_of(c * 256, 256), 256)
        for n in range(NB):
            in_t[n, :, rows] = in_v[rows, lanes(n)].T
            cot_t[n, :, rows] = cot_v[rows, lanes(n)].T

    def columns(rc, x):
        @pl.loop(0, 8)
        def _(c):
            rows = pl.ds(pl.multiple_of(c * 256, 256), 256)
            for n in range(NB):
                xs[n, rows, :] = rc[pl.ds(c * 8, 8), :, lanes(n)].reshape(256, 128).astype(F32)

        for k in range(KD):
            for n in range(NB):
                x[k, :, lanes(n)] = xs[n, pl.ds(k, N1, stride=KD), :].astype(BF16)

    def product(lhs, x, slab):
        for k in range(KD):
            y = nn(lhs[...], x[k])
            for n in range(NB):
                xs[n, pl.ds(k, N1, stride=KD), :] = y[:, lanes(n)]

        @pl.loop(0, 8)
        def _(c):
            rows = pl.ds(pl.multiple_of(c * 256, 256), 256)
            for n in range(NB):
                slab(c, n)[...] = xs[n, rows, :].astype(BF16).reshape(8, LOC * KD, 128)

    wait_slots(rc_g, rcv.at[0])
    columns(rc_g, x_g)
    product(fb, x_g, lambda c, n: sr_g.at[pl.ds(c * 8, 8), :, lanes(n)])
    send_all(lambda d: sr_g.at[d], rr_g, 2)
    rr_g[me] = sr_g[me]

    wait_slots(rc_f, rcv.at[1])
    columns(rc_f, x_f)
    product(b_t, x_f, lambda c, n: sr_f.at[n, pl.ds(c * 8, 8)])
    for n in range(NB):
        send_all(lambda d, n=n: sr_f.at[n, d], rr_f.at[n], 3 + n)
    for n in range(NB):
        rr_f[n, me] = sr_f[n, me]

    fb_acc[...] = nt(x_f[0], x_g[0])

    @pl.loop(1, KD)
    def _(k):
        fb_acc[...] += nt(x_f[k], x_g[k])

    for h in range(2):
        r1s[:, h, :, 512:640] = fb_acc[:, lanes(h)].reshape(TM // 2, 8, 128)

    wait_slots(rr_g, rcv.at[2])

    @pl.loop(0, N2 // CR)
    def _(c):
        for n in range(NB):
            gt = by_block(
                rr_g[pl.ds(c * DC, DC), :, lanes(n)].reshape(LOC * CR, 128).astype(F32)
            )
            gf = (gt * four(ker_v, c, n).astype(F32)).astype(BF16)
            gk = (gt * four(first_v, c, n)).astype(BF16)
            put_four(gf_v, c, n, gf)
            put_four(gker_v, c, n, gk)

    fa_acc[...] = jnp.zeros_like(fa_acc)

    @pl.loop(0, LOC)
    def _(i):
        rows = pl.ds(pl.multiple_of(i * N2, N2), N2)
        gm_v[rows, :] = nn(fa[...], gf_v[rows, :]).astype(BF16)
        fa_acc[...] += nt(mx_v[rows, :], gf_v[rows, :])

    r1s[:, :, :, 0:512] = fa_acc[...].reshape(TM // 2, 2, 8, 512)
    for n in range(NB):
        r1s[n * 8 : (n + 1) * 8, :, :, 640:768] = nn(in_t[n], gm_v[:, lanes(n)]).reshape(
            8, 2, 8, 128
        )
    r1s[24:32, :, :, 640:768] = jnp.zeros((8, 2, 8, 128), F32)
    half = copy_to(r1s.at[:, 1 - core], rp, 9, (me ^ 1, te))
    half.start()

    def forward_tail(n):
        wait_slots(rr_f.at[n], rcv.at[3 + n])

        @pl.loop(0, N2 // CR)
        def _(c):
            sec = by_block(
                rr_f[n, pl.ds(c * DC, DC)].reshape(LOC * CR, 128).astype(F32)
            )
            put_four(gated_v, c, n, (sec * four(gate_v, c, n)).astype(BF16))
            put_four(ggate_v, c, n, (sec * four(gg_v, c, n)).astype(BF16))

        r2s[n, 0:16] = nn(in_t[n], ggate_v[:, lanes(n)]).reshape(16, 8, 128).astype(BF16)
        r2s[n, 16:32] = nn(cot_t[n], gated_v[:, lanes(n)]).T.reshape(16, 8, 128).astype(BF16)
        own = n % 2

        def send(d):
            @pl.when((d & 1) == own)
            def _():
                copy_to(r2s.at[n, d >> 1], r2r.at[n, me], 11 + n, (d, te)).start()

        each_peer(send)

        @pl.when(core == own)
        def _():
            r2r[n, me] = r2s[n, chip]

    forward_tail(0)
    half.wait_recv()

    @pl.loop(0, TM // 2)
    def _(g):
        both = rp[g] + r1s[g, core]
        r1b[g] = jnp.concatenate([both[:, 0:CH], both[:, CH:]], axis=0).astype(BF16)

    each_peer(
        lambda d: copy_to(r1b.at[d >> 1], r1r.at[chip], 6, (d, te)).start(), cores=(0,)
    )
    r1r[chip] = r1b[chip]
    forward_tail(1)
    forward_tail(2)

    @pl.loop(0, ROWS // 256)
    def _(c):
        rows = pl.ds(pl.multiple_of(c * 256, 256), 256)
        for n in range(NB):
            out_v[rows, lanes(n)] = nn(gated_v[rows, lanes(n)], w_out[n]).astype(BF16)
            gin_v[rows, lanes(n)] = (
                nt(gm_v[rows, lanes(n)], w_in[n]) + nt(ggate_v[rows, lanes(n)], w_gate[n])
            ).astype(BF16)

    def four_slots(q):
        a, b, c, d = (r1r[q * 4 + j].astype(F32) for j in range(4))
        return (a + b) + (c + d)

    token_scale = 1.0 / math.sqrt(N1 * N2)
    wait_slots(r1r, rcv.at[6], TM // 2 - 1)
    sum1 = lax.fori_loop(0, TM // 8, lambda q, acc: acc + four_slots(q), jnp.zeros((16, CH), F32))
    tr[te, :, 0:CH] = sum1[0:8]
    tr[te, :, CH:640] = sum1[8:16, 0:256]
    for q in range(1, TE):
        copy_to(tr.at[te], tr.at[te], 7, (me, lax.rem(te + q, TE))).start()

    def to_chips(piece, ph):
        each_peer(lambda d: copy_to(piece, piece, ph, (d, te)).start(), cores=(0,))

    @pl.when(me < OWN)
    def _():
        ag1[chip, core] = sum1[8:16, 256:CH] * token_scale
        to_chips(ag1.at[chip, core], 10)

    for n in range(NB):

        @pl.when(core == n % 2)
        def _(n=n):
            wait_slots(r2r.at[n], rcv.at[11 + n])
            ag2[n, chip] = jnp.sum(r2r[n].astype(F32), axis=0) * token_scale
            if n < NB - 1:
                to_chips(ag2.at[n, chip], 14 + n)
            else:
                piece = ag2.at[n, chip]
                each_peer(lambda d: copy_to(piece, piece, 14 + n, (d, te)).start())

    wait_slots(tr, rcv.at[7], TE - 1)
    total = tr[0] + tr[1] + tr[2] + tr[3]
    gfa[...] = total[:, 0:512] * (1.0 / math.sqrt(N1 * D))
    pr[core] = total[:, 512:640] * (1.0 / math.sqrt(N2 * D))
    pair = copy_to(pr.at[core], pr.at[core], 8, (me ^ 1, te))
    pair.start()

    def either(cond, then, other):
        @pl.when(cond)
        def _():
            then()

        @pl.when(jnp.logical_not(cond))
        def _():
            other()

    other = (me ^ 1, te)
    either(
        me < OWN,
        lambda: wait_slots(ag2.at[0], rcv.at[10], OWN // 2 - 1),
        lambda: wait_slots(ag2.at[0], rcv.at[10], OWN // 2),
    )
    pass1 = copy_to(ag1.at[:, core], ag1.at[:, core], 17, other)
    pass1.start()
    for n in range(NB - 1):

        @pl.when(core == n % 2)
        def _(n=n):
            wait_slots(ag2.at[n], rcv.at[14 + n], TM // 2 - 1)
            copy_to(ag2.at[n], ag2.at[n], 18 + n, other).start()

    pair.wait()
    for h in range(2):
        gfb[:, lanes(h)] = jnp.where(core == 0, pr[h, 0:4, :], pr[h, 4:8, :])

    pass1.wait_recv()
    gw_in[...] = ag1[...].reshape(OWN, 8, 128)
    for n in range(NB):

        if n < NB - 1:

            @pl.when(core != n % 2)
            def _(n=n):
                wait_slots(ag2.at[n], rcv.at[18 + n], TM // 2)

        else:
            either(
                core == n % 2,
                lambda: wait_slots(ag2.at[n], rcv.at[14 + n], TM // 2 - 1),
                lambda: wait_slots(ag2.at[n], rcv.at[14 + n], TM // 2),
            )
        gw_gate[n * 16 : (n + 1) * 16] = ag2[n, 0:16]
        gw_out[n * 16 : (n + 1) * 16] = ag2[n, 16:32]

    wait_slots(rc_g, snd.at[0])
    wait_slots(rc_f, snd.at[1])
    wait_slots(rr_g, snd.at[2])
    for n in range(NB):
        wait_slots(rr_f.at[n], snd.at[3 + n])
        either(
            core == n % 2,
            lambda: wait_slots(r2r.at[n], snd.at[11 + n], TM // 2 - 1),
            lambda: wait_slots(r2r.at[n], snd.at[11 + n], TM // 2),
        )

        @pl.when(core == n % 2)
        def _(n=n):
            if n < NB - 1:
                wait_slots(ag2.at[n], snd.at[14 + n], TM // 2 - 1)
                wait_slots(ag2.at[n], snd.at[18 + n], TM // 2)
            else:
                wait_slots(ag2.at[n], snd.at[14 + n], TM // 2)
                wait_slots(ag2.at[n], snd.at[14 + n], TM // 2 - 1)

    wait_slots(r1r, snd.at[6], TM // 2 - 1)
    wait_slots(tr, snd.at[7], TE - 1)
    half.wait_send()
    pass1.wait_send()

    @pl.when(me < OWN)
    def _():
        wait_slots(ag2.at[0], snd.at[10], TM // 2 - 1)


def finish_body(*refs):
    srcs, dsts, sem = refs[:8], refs[8:16], refs[16]
    stores = []
    for src, dst in zip(srcs, dsts, strict=True):
        cuts = 4 if src.shape[0] == ROWS else 1
        step = src.shape[0] // cuts
        for j in range(cuts):
            rows = pl.ds(j * step, step)
            stores.append(pltpu.make_async_copy(src.at[rows], dst.at[rows], sem.at[len(stores)]))
    for cp in stores:
        cp.start()
    for cp in stores:
        cp.wait()


def body(inputs, kernel, w_in, w_gate, w_out, factor_a, factor_b, cotangent):
    any_spec = pl.BlockSpec(memory_space=pl.ANY)
    vm = pl.BlockSpec(memory_space=pltpu.VMEM)
    wide = pltpu.VMEM((ROWS, CH), F32)
    act = pltpu.VMEM((ROWS, CH), BF16)
    turned = pltpu.VMEM((NB, 128, ROWS), BF16)
    slots = pltpu.VMEM((TM, LOC * KD, CH), BF16)
    mixer = pltpu.VMEM((NB, 128, 128), BF16)
    slots_n = pltpu.VMEM((NB, TM, LOC * KD, 128), BF16)
    cols = pltpu.VMEM((KD, N1, CH), BF16)
    tile = pltpu.VMEM((OWN, 8, 128), F32)
    outs = pl.pallas_call(
        kernel_body,
        name="monarch",
        out_shape=(
            act,
            act,
            act,
            tile,
            tile,
            tile,
            pltpu.VMEM((8, N2), F32),
            pltpu.VMEM((4, N1), F32),
        ),
        in_specs=[any_spec] * 8,
        out_specs=(vm,) * 8,
        scratch_shapes=[
            act,
            act,
            act,
            mixer,
            mixer,
            mixer,
            pltpu.VMEM((N2, N2), BF16),
            pltpu.VMEM((N1, N1), BF16),
            turned,
            turned,
            pltpu.VMEM((N2, N2), BF16),
            pltpu.VMEM((N1, N1), BF16),
            wide,
            wide,
            wide,
            act,
            slots,
            slots,
            slots,
            slots,
            pltpu.VMEM((NB, ROWS, 128), F32),
            cols,
            cols,
            slots,
            slots_n,
            slots,
            slots_n,
            act,
            act,
            act,
            act,
            pltpu.VMEM((N1, N1), F32),
            pltpu.VMEM((N2, N2), F32),
            pltpu.VMEM((TM // 2, 2, 8, 768), F32),
            pltpu.VMEM((TM // 2, 16, CH), BF16),
            pltpu.VMEM((TM // 2, 16, CH), BF16),
            pltpu.VMEM((TM // 2, 8, 768), F32),
            pltpu.VMEM((NB, TM // 2, 8, 128), BF16),
            pltpu.VMEM((NB, TM, 8, 128), BF16),
            pltpu.VMEM((TE, 8, 640), F32),
            pltpu.VMEM((2, 8, 128), F32),
            pltpu.VMEM((OWN // 2, 2, 8, 128), F32),
            pltpu.VMEM((NB, TM // 2, 8, 128), F32),
            pltpu.SemaphoreType.DMA((8,)),
            pltpu.SemaphoreType.DMA((21,)),
            pltpu.SemaphoreType.DMA((21,)),
        ],
        compiler_params=pltpu.CompilerParams(
            collective_id=0, has_side_effects=True, vmem_limit_bytes=57 << 20
        ),
    )(inputs, kernel, w_in, w_gate, w_out, factor_a, factor_b, cotangent)
    outs = pl.pallas_call(
        finish_body,
        name="finish",
        out_shape=tuple(jax.ShapeDtypeStruct(o.shape, o.dtype) for o in outs),
        in_specs=[vm] * len(outs),
        out_specs=(any_spec,) * len(outs),
        scratch_shapes=[pltpu.SemaphoreType.DMA((17,))],
        compiler_params=pltpu.CompilerParams(vmem_limit_bytes=8 << 20),
    )(*outs)
    out, gin, gker, gwi, gwg, gwo, gfa, gfb = outs
    shape = (NB, 128, 128)
    return (
        out,
        gin,
        gker,
        gwi.reshape(shape),
        gwg.reshape(shape),
        gwo.reshape(shape),
        gfa,
        gfb,
    )


def solution(mesh):
    return jax.shard_map(
        body,
        mesh=mesh,
        in_specs=(
            P("tm", "tensor"),
            P("tm", "tensor"),
            P("tensor", None, None),
            P("tensor", None, None),
            P("tensor", None, None),
            P(),
            P(),
            P("tm", "tensor"),
        ),
        out_specs=(
            P("tm", "tensor"),
            P("tm", "tensor"),
            P("tm", "tensor"),
            P("tensor", None, None),
            P("tensor", None, None),
            P("tensor", None, None),
            P("tm", None),
            P("tm", None),
        ),
        check_vma=False,
    )
```

```python
import math

import jax
import jax.numpy as jnp
from jax import lax
from jax.experimental import pallas as pl
from jax.experimental.pallas import tpu as pltpu
from jax.sharding import PartitionSpec as P

D = 1536
N1 = 256
N2 = 512
MESH = pl.DeviceIdType.MESH
F32 = jnp.float32
BF16 = jnp.bfloat16
TM = 64
TE = 4
ROWS = 2048
CH = 384
LOC = 4
KD = 8
NB = 3
OWN = 48
DC = 8
CR = DC * KD


def lanes(n):
    return slice(n * 128, (n + 1) * 128)


def nt(a, b):
    return lax.dot_general(a, b, (((1,), (1,)), ((), ())), preferred_element_type=F32)


def nn(a, b):
    return jnp.dot(a, b, preferred_element_type=F32)


def four(ref, c, n):
    return jnp.concatenate(
        [ref[pl.ds(i * N2 + c * CR, CR), lanes(n)] for i in range(LOC)], axis=0
    )


def put_four(ref, c, n, val):
    for i in range(LOC):
        ref[pl.ds(i * N2 + c * CR, CR), lanes(n)] = val[i * CR : (i + 1) * CR]


def by_dest(val):
    return jnp.concatenate(
        [
            val[i * CR + d * KD : i * CR + (d + 1) * KD]
            for d in range(DC)
            for i in range(LOC)
        ],
        axis=0,
    )


def by_block(val):
    return jnp.concatenate(
        [
            val[(d * LOC + i) * KD : (d * LOC + i + 1) * KD]
            for i in range(LOC)
            for d in range(DC)
        ],
        axis=0,
    )


def kernel_body(
    in_h,
    ker_h,
    wi_h,
    wg_h,
    wo_h,
    fa_h,
    fb_h,
    cot_h,
    out_v,
    gin_v,
    gker_v,
    gw_in,
    gw_gate,
    gw_out,
    gfa,
    gfb,
    in_v,
    ker_v,
    cot_v,
    w_in,
    w_gate,
    w_out,
    fa,
    fb,
    in_t,
    cot_t,
    a_t,
    b_t,
    gate_v,
    gg_v,
    first_v,
    mx_v,
    so_g,
    so_f,
    rc_g,
    rc_f,
    xs,
    x_g,
    x_f,
    sr_g,
    sr_f,
    rr_g,
    rr_f,
    gf_v,
    gm_v,
    gated_v,
    ggate_v,
    fb_acc,
    fa_acc,
    r1s,
    r1r,
    r1b,
    rp,
    r2s,
    r2r,
    tr,
    pr,
    ag1,
    ag2,
    ld_sem,
    snd,
    rcv,
):
    me = lax.axis_index("tm")
    te = lax.axis_index("tensor")
    core = me & 1
    my = (me >> 1) & 3
    mx = (me >> 3) & 3
    mz = me >> 5
    chip = me >> 1

    def each_peer(fn, cores=(0, 1)):
        for dz, dc in ((1, 1), (0, 1), (1, 0), (0, 0)):
            if dc in cores:
                here = dz + dc == 0

                @pl.loop(int(here), 16, unroll=3 if here else 4)
                def _(p, dz=dz, dc=dc):
                    q = (p * 5) & 15
                    x = (mx + (q >> 2)) & 3
                    y = (my + q) & 3
                    fn((((mz ^ dz) * 4 + x) * 4 + y) * 2 + (core ^ dc))

    loads = [
        pltpu.make_async_copy(src, dst, ld_sem.at[j])
        for j, (src, dst) in enumerate(
            (
                (wg_h, w_gate),
                (wo_h, w_out),
                (cot_h, cot_v),
                (in_h, in_v),
                (wi_h, w_in),
                (fa_h, fa),
                (ker_h, ker_v),
                (fb_h, fb),
            )
        )
    ]
    for cp in loads:
        cp.start()

    barrier = pltpu.get_barrier_semaphore()

    each_peer(
        lambda d: pl.semaphore_signal(barrier, inc=1, device_id=(d, te), device_id_type=MESH)
    )

    for q in range(1, TE):
        pl.semaphore_signal(
            barrier, inc=1, device_id=(me, lax.rem(te + q, TE)), device_id_type=MESH
        )

    def copy_to(src, dst, ph, device):
        return pltpu.make_async_remote_copy(
            src_ref=src,
            dst_ref=dst,
            send_sem=snd.at[ph],
            recv_sem=rcv.at[ph],
            device_id=device,
            device_id_type=MESH,
        )

    def send_all(slot_of, dst, ph):
        each_peer(lambda d: copy_to(slot_of(d), dst.at[me], ph, (d, te)).start())

    def wait_slots(ref, sem, slots=TM - 1):
        part = ref.at[pl.ds(0, slots)]
        pltpu.make_async_copy(part, part, sem).wait()

    for cp in loads[:4]:
        cp.wait()

    @pl.loop(0, N2 // CR)
    def _(c):
        for n in range(NB):
            gate = nn(four(in_v, c, n), w_gate[n])
            gg = nt(four(cot_v, c, n), w_out[n])
            put_four(gate_v, c, n, gate)
            put_four(gg_v, c, n, gg)
            so_g[pl.ds(c * DC, DC), :, lanes(n)] = (
                by_dest(gate * gg).astype(BF16).reshape(DC, LOC * KD, 128)
            )

    pl.semaphore_wait(barrier, TM - 1 + TE - 1)
    send_all(lambda d: so_g.at[d], rc_g, 0)

    loads[4].wait()
    loads[5].wait()
    for s in range(4):
        a_t[:, lanes(s)] = fa[lanes(s), :].T

    @pl.loop(0, LOC)
    def _(i):
        rows = pl.ds(pl.multiple_of(i * N2, N2), N2)
        for n in range(NB):
            mx_v[rows, lanes(n)] = nn(in_v[rows, lanes(n)], w_in[n]).astype(BF16)
        first_v[rows, :] = nn(a_t[...], mx_v[rows, :])

    loads[6].wait()

    @pl.loop(0, N2 // CR)
    def _(c):
        for n in range(NB):
            tw = four(first_v, c, n) * four(ker_v, c, n).astype(F32)
            so_f[pl.ds(c * DC, DC), :, lanes(n)] = (
                by_dest(tw).astype(BF16).reshape(DC, LOC * KD, 128)
            )

    send_all(lambda d: so_f.at[d], rc_f, 1)
    rc_g[me] = so_g[me]
    rc_f[me] = so_f[me]

    loads[7].wait()
    b_t[...] = fb[...].T

    @pl.loop(0, ROWS // 256)
    def _(c):
        rows = pl.ds(pl.multiple_of(c * 256, 256), 256)
        for n in range(NB):
            in_t[n, :, rows] = in_v[rows, lanes(n)].T
            cot_t[n, :, rows] = cot_v[rows, lanes(n)].T

    def columns(rc, x):
        @pl.loop(0, 8)
        def _(c):
            rows = pl.ds(pl.multiple_of(c * 256, 256), 256)
            for n in range(NB):
                xs[n, rows, :] = rc[pl.ds(c * 8, 8), :, lanes(n)].reshape(256, 128).astype(F32)

        for k in range(KD):
            for n in range(NB):
                x[k, :, lanes(n)] = xs[n, pl.ds(k, N1, stride=KD), :].astype(BF16)

    def product(lhs, x, slab):
        for k in range(KD):
            y = nn(lhs[...], x[k])
            for n in range(NB):
                xs[n, pl.ds(k, N1, stride=KD), :] = y[:, lanes(n)]

        @pl.loop(0, 8)
        def _(c):
            rows = pl.ds(pl.multiple_of(c * 256, 256), 256)
            for n in range(NB):
                slab(c, n)[...] = xs[n, rows, :].astype(BF16).reshape(8, LOC * KD, 128)

    wait_slots(rc_g, rcv.at[0])
    columns(rc_g, x_g)
    product(fb, x_g, lambda c, n: sr_g.at[pl.ds(c * 8, 8), :, lanes(n)])
    send_all(lambda d: sr_g.at[d], rr_g, 2)
    rr_g[me] = sr_g[me]

    wait_slots(rc_f, rcv.at[1])
    columns(rc_f, x_f)
    product(b_t, x_f, lambda c, n: sr_f.at[n, pl.ds(c * 8, 8)])
    for n in range(NB):
        send_all(lambda d, n=n: sr_f.at[n, d], rr_f.at[n], 3 + n)
    for n in range(NB):
        rr_f[n, me] = sr_f[n, me]

    fb_acc[...] = nt(x_f[0], x_g[0])

    @pl.loop(1, KD)
    def _(k):
        fb_acc[...] += nt(x_f[k], x_g[k])

    for h in range(2):
        r1s[:, h, :, 512:640] = fb_acc[:, lanes(h)].reshape(TM // 2, 8, 128)

    wait_slots(rr_g, rcv.at[2])

    @pl.loop(0, N2 // CR)
    def _(c):
        for n in range(NB):
            gt = by_block(
                rr_g[pl.ds(c * DC, DC), :, lanes(n)].reshape(LOC * CR, 128).astype(F32)
            )
            gf = (gt * four(ker_v, c, n).astype(F32)).astype(BF16)
            gk = (gt * four(first_v, c, n)).astype(BF16)
            put_four(gf_v, c, n, gf)
            put_four(gker_v, c, n, gk)

    fa_acc[...] = jnp.zeros_like(fa_acc)

    @pl.loop(0, LOC)
    def _(i):
        rows = pl.ds(pl.multiple_of(i * N2, N2), N2)
        gm_v[rows, :] = nn(fa[...], gf_v[rows, :]).astype(BF16)
        fa_acc[...] += nt(mx_v[rows, :], gf_v[rows, :])

    r1s[:, :, :, 0:512] = fa_acc[...].reshape(TM // 2, 2, 8, 512)
    for n in range(NB):
        r1s[n * 8 : (n + 1) * 8, :, :, 640:768] = nn(in_t[n], gm_v[:, lanes(n)]).reshape(
            8, 2, 8, 128
        )
    r1s[24:32, :, :, 640:768] = jnp.zeros((8, 2, 8, 128), F32)
    half = copy_to(r1s.at[:, 1 - core], rp, 9, (me ^ 1, te))
    half.start()

    def forward_tail(n):
        wait_slots(rr_f.at[n], rcv.at[3 + n])

        @pl.loop(0, N2 // CR)
        def _(c):
            sec = by_block(
                rr_f[n, pl.ds(c * DC, DC)].reshape(LOC * CR, 128).astype(F32)
            )
            put_four(gated_v, c, n, (sec * four(gate_v, c, n)).astype(BF16))
            put_four(ggate_v, c, n, (sec * four(gg_v, c, n)).astype(BF16))

        r2s[n, 0:16] = nn(in_t[n], ggate_v[:, lanes(n)]).reshape(16, 8, 128).astype(BF16)
        r2s[n, 16:32] = nn(cot_t[n], gated_v[:, lanes(n)]).T.reshape(16, 8, 128).astype(BF16)
        own = n % 2

        def send(d):
            @pl.when((d & 1) == own)
            def _():
                copy_to(r2s.at[n, d >> 1], r2r.at[n, me], 11 + n, (d, te)).start()

        each_peer(send)

        @pl.when(core == own)
        def _():
            r2r[n, me] = r2s[n, chip]

    forward_tail(0)
    half.wait_recv()

    @pl.loop(0, TM // 2)
    def _(g):
        both = rp[g] + r1s[g, core]
        r1b[g] = jnp.concatenate([both[:, 0:CH], both[:, CH:]], axis=0).astype(BF16)

    each_peer(
        lambda d: copy_to(r1b.at[d >> 1], r1r.at[chip], 6, (d, te)).start(), cores=(0,)
    )
    r1r[chip] = r1b[chip]
    forward_tail(1)
    forward_tail(2)

    @pl.loop(0, ROWS // 256)
    def _(c):
        rows = pl.ds(pl.multiple_of(c * 256, 256), 256)
        for n in range(NB):
            out_v[rows, lanes(n)] = nn(gated_v[rows, lanes(n)], w_out[n]).astype(BF16)
            gin_v[rows, lanes(n)] = (
                nt(gm_v[rows, lanes(n)], w_in[n]) + nt(ggate_v[rows, lanes(n)], w_gate[n])
            ).astype(BF16)

    def four_slots(q):
        a, b, c, d = (r1r[q * 4 + j].astype(F32) for j in range(4))
        return (a + b) + (c + d)

    token_scale = 1.0 / math.sqrt(N1 * N2)
    wait_slots(r1r, rcv.at[6], TM // 2 - 1)
    sum1 = lax.fori_loop(0, TM // 8, lambda q, acc: acc + four_slots(q), jnp.zeros((16, CH), F32))
    tr[te, :, 0:CH] = sum1[0:8]
    tr[te, :, CH:640] = sum1[8:16, 0:256]
    for q in range(1, TE):
        copy_to(tr.at[te], tr.at[te], 7, (me, lax.rem(te + q, TE))).start()

    def to_chips(piece, ph):
        each_peer(lambda d: copy_to(piece, piece, ph, (d, te)).start(), cores=(0,))

    @pl.when(me < OWN)
    def _():
        ag1[chip, core] = sum1[8:16, 256:CH] * token_scale
        to_chips(ag1.at[chip, core], 10)

    for n in range(NB):

        @pl.when(core == n % 2)
        def _(n=n):
            wait_slots(r2r.at[n], rcv.at[11 + n])
            ag2[n, chip] = jnp.sum(r2r[n].astype(F32), axis=0) * token_scale
            if n < NB - 1:
                to_chips(ag2.at[n, chip], 14 + n)
            else:
                piece = ag2.at[n, chip]
                each_peer(lambda d: copy_to(piece, piece, 14 + n, (d, te)).start())

    def either(cond, then, other):
        @pl.when(cond)
        def _():
            then()

        @pl.when(jnp.logical_not(cond))
        def _():
            other()

    other = (me ^ 1, te)
    either(
        me < OWN,
        lambda: wait_slots(ag2.at[0], rcv.at[10], OWN // 2 - 1),
        lambda: wait_slots(ag2.at[0], rcv.at[10], OWN // 2),
    )
    pass1 = copy_to(ag1.at[:, core], ag1.at[:, core], 17, other)
    pass1.start()
    for n in range(NB - 1):

        @pl.when(core == n % 2)
        def _(n=n):
            wait_slots(ag2.at[n], rcv.at[14 + n], TM // 2 - 1)
            copy_to(ag2.at[n], ag2.at[n], 18 + n, other).start()

    wait_slots(tr, rcv.at[7], TE - 1)
    total = tr[0] + tr[1] + tr[2] + tr[3]
    gfa[...] = total[:, 0:512] * (1.0 / math.sqrt(N1 * D))
    pr[core] = total[:, 512:640] * (1.0 / math.sqrt(N2 * D))
    pair = copy_to(pr.at[core], pr.at[core], 8, (me ^ 1, te))
    pair.start()

    pass1.wait_recv()
    gw_in[...] = ag1[...].reshape(OWN, 8, 128)
    for n in range(NB):

        if n < NB - 1:

            @pl.when(core != n % 2)
            def _(n=n):
                wait_slots(ag2.at[n], rcv.at[18 + n], TM // 2)

        else:
            either(
                core == n % 2,
                lambda: wait_slots(ag2.at[n], rcv.at[14 + n], TM // 2 - 1),
                lambda: wait_slots(ag2.at[n], rcv.at[14 + n], TM // 2),
            )
        gw_gate[n * 16 : (n + 1) * 16] = ag2[n, 0:16]
        gw_out[n * 16 : (n + 1) * 16] = ag2[n, 16:32]

    pair.wait()
    for h in range(2):
        gfb[:, lanes(h)] = jnp.where(core == 0, pr[h, 0:4, :], pr[h, 4:8, :])

    wait_slots(rc_g, snd.at[0])
    wait_slots(rc_f, snd.at[1])
    wait_slots(rr_g, snd.at[2])
    for n in range(NB):
        wait_slots(rr_f.at[n], snd.at[3 + n])
        either(
            core == n % 2,
            lambda: wait_slots(r2r.at[n], snd.at[11 + n], TM // 2 - 1),
            lambda: wait_slots(r2r.at[n], snd.at[11 + n], TM // 2),
        )

        @pl.when(core == n % 2)
        def _(n=n):
            if n < NB - 1:
                wait_slots(ag2.at[n], snd.at[14 + n], TM // 2 - 1)
                wait_slots(ag2.at[n], snd.at[18 + n], TM // 2)
            else:
                wait_slots(ag2.at[n], snd.at[14 + n], TM // 2)
                wait_slots(ag2.at[n], snd.at[14 + n], TM // 2 - 1)

    wait_slots(r1r, snd.at[6], TM // 2 - 1)
    wait_slots(tr, snd.at[7], TE - 1)
    half.wait_send()
    pass1.wait_send()

    @pl.when(me < OWN)
    def _():
        wait_slots(ag2.at[0], snd.at[10], TM // 2 - 1)


def finish_body(*refs):
    srcs, dsts, sem = refs[:8], refs[8:16], refs[16]
    stores = []
    for src, dst in zip(srcs, dsts, strict=True):
        cuts = 4 if src.shape[0] == ROWS else 1
        step = src.shape[0] // cuts
        for j in range(cuts):
            rows = pl.ds(j * step, step)
            stores.append(pltpu.make_async_copy(src.at[rows], dst.at[rows], sem.at[len(stores)]))
    for cp in stores:
        cp.start()
    for cp in stores:
        cp.wait()


def body(inputs, kernel, w_in, w_gate, w_out, factor_a, factor_b, cotangent):
    any_spec = pl.BlockSpec(memory_space=pl.ANY)
    vm = pl.BlockSpec(memory_space=pltpu.VMEM)
    wide = pltpu.VMEM((ROWS, CH), F32)
    act = pltpu.VMEM((ROWS, CH), BF16)
    turned = pltpu.VMEM((NB, 128, ROWS), BF16)
    slots = pltpu.VMEM((TM, LOC * KD, CH), BF16)
    mixer = pltpu.VMEM((NB, 128, 128), BF16)
    slots_n = pltpu.VMEM((NB, TM, LOC * KD, 128), BF16)
    cols = pltpu.VMEM((KD, N1, CH), BF16)
    tile = pltpu.VMEM((OWN, 8, 128), F32)
    outs = pl.pallas_call(
        kernel_body,
        name="monarch",
        out_shape=(
            act,
            act,
            act,
            tile,
            tile,
            tile,
            pltpu.VMEM((8, N2), F32),
            pltpu.VMEM((4, N1), F32),
        ),
        in_specs=[any_spec] * 8,
        out_specs=(vm,) * 8,
        scratch_shapes=[
            act,
            act,
            act,
            mixer,
            mixer,
            mixer,
            pltpu.VMEM((N2, N2), BF16),
            pltpu.VMEM((N1, N1), BF16),
            turned,
            turned,
            pltpu.VMEM((N2, N2), BF16),
            pltpu.VMEM((N1, N1), BF16),
            wide,
            wide,
            wide,
            act,
            slots,
            slots,
            slots,
            slots,
            pltpu.VMEM((NB, ROWS, 128), F32),
            cols,
            cols,
            slots,
            slots_n,
            slots,
            slots_n,
            act,
            act,
            act,
            act,
            pltpu.VMEM((N1, N1), F32),
            pltpu.VMEM((N2, N2), F32),
            pltpu.VMEM((TM // 2, 2, 8, 768), F32),
            pltpu.VMEM((TM // 2, 16, CH), BF16),
            pltpu.VMEM((TM // 2, 16, CH), BF16),
            pltpu.VMEM((TM // 2, 8, 768), F32),
            pltpu.VMEM((NB, TM // 2, 8, 128), BF16),
            pltpu.VMEM((NB, TM, 8, 128), BF16),
            pltpu.VMEM((TE, 8, 640), F32),
            pltpu.VMEM((2, 8, 128), F32),
            pltpu.VMEM((OWN // 2, 2, 8, 128), F32),
            pltpu.VMEM((NB, TM // 2, 8, 128), F32),
            pltpu.SemaphoreType.DMA((8,)),
            pltpu.SemaphoreType.DMA((21,)),
            pltpu.SemaphoreType.DMA((21,)),
        ],
        compiler_params=pltpu.CompilerParams(
            collective_id=0, has_side_effects=True, vmem_limit_bytes=57 << 20
        ),
    )(inputs, kernel, w_in, w_gate, w_out, factor_a, factor_b, cotangent)
    outs = pl.pallas_call(
        finish_body,
        name="finish",
        out_shape=tuple(jax.ShapeDtypeStruct(o.shape, o.dtype) for o in outs),
        in_specs=[vm] * len(outs),
        out_specs=(any_spec,) * len(outs),
        scratch_shapes=[pltpu.SemaphoreType.DMA((17,))],
        compiler_params=pltpu.CompilerParams(vmem_limit_bytes=8 << 20),
    )(*outs)
    out, gin, gker, gwi, gwg, gwo, gfa, gfb = outs
    shape = (NB, 128, 128)
    return (
        out,
        gin,
        gker,
        gwi.reshape(shape),
        gwg.reshape(shape),
        gwo.reshape(shape),
        gfa,
        gfb,
    )


def solution(mesh):
    return jax.shard_map(
        body,
        mesh=mesh,
        in_specs=(
            P("tm", "tensor"),
            P("tm", "tensor"),
            P("tensor", None, None),
            P("tensor", None, None),
            P("tensor", None, None),
            P(),
            P(),
            P("tm", "tensor"),
        ),
        out_specs=(
            P("tm", "tensor"),
            P("tm", "tensor"),
            P("tm", "tensor"),
            P("tensor", None, None),
            P("tensor", None, None),
            P("tensor", None, None),
            P("tm", None),
            P("tm", None),
        ),
        check_vma=False,
    )
```

```python
import math

import jax
import jax.numpy as jnp
from jax import lax
from jax.experimental import pallas as pl
from jax.experimental.pallas import tpu as pltpu
from jax.sharding import PartitionSpec as P

D = 1536
N1 = 256
N2 = 512
MESH = pl.DeviceIdType.MESH
F32 = jnp.float32
BF16 = jnp.bfloat16
TM = 64
TE = 4
ROWS = 2048
CH = 384
LOC = 4
KD = 8
NB = 3
OWN = 48
DC = 8
CR = DC * KD


def lanes(n):
    return slice(n * 128, (n + 1) * 128)


def nt(a, b):
    return lax.dot_general(a, b, (((1,), (1,)), ((), ())), preferred_element_type=F32)


def nn(a, b):
    return jnp.dot(a, b, preferred_element_type=F32)


def four(ref, c, n):
    return jnp.concatenate(
        [ref[pl.ds(i * N2 + c * CR, CR), lanes(n)] for i in range(LOC)], axis=0
    )


def put_four(ref, c, n, val):
    for i in range(LOC):
        ref[pl.ds(i * N2 + c * CR, CR), lanes(n)] = val[i * CR : (i + 1) * CR]


def by_dest(val):
    return jnp.concatenate(
        [
            val[i * CR + d * KD : i * CR + (d + 1) * KD]
            for d in range(DC)
            for i in range(LOC)
        ],
        axis=0,
    )


def by_block(val):
    return jnp.concatenate(
        [
            val[(d * LOC + i) * KD : (d * LOC + i + 1) * KD]
            for i in range(LOC)
            for d in range(DC)
        ],
        axis=0,
    )


def kernel_body(
    in_h,
    ker_h,
    wi_h,
    wg_h,
    wo_h,
    fa_h,
    fb_h,
    cot_h,
    out_v,
    gin_v,
    gker_v,
    gw_in,
    gw_gate,
    gw_out,
    gfa,
    gfb,
    in_v,
    ker_v,
    cot_v,
    w_in,
    w_gate,
    w_out,
    fa,
    fb,
    in_t,
    cot_t,
    a_t,
    b_t,
    gate_v,
    gg_v,
    first_v,
    mx_v,
    so_g,
    so_f,
    rc_g,
    rc_f,
    xs,
    x_g,
    x_f,
    sr_g,
    sr_f,
    rr_g,
    rr_f,
    gf_v,
    gm_v,
    gated_v,
    ggate_v,
    fb_acc,
    fa_acc,
    r1s,
    r1r,
    r1b,
    rp,
    r2s,
    r2r,
    tr,
    pr,
    ag1,
    ag2,
    ld_sem,
    snd,
    rcv,
):
    me = lax.axis_index("tm")
    te = lax.axis_index("tensor")
    core = me & 1
    my = (me >> 1) & 3
    mx = (me >> 3) & 3
    mz = me >> 5
    chip = me >> 1

    def each_peer(fn, cores=(0, 1)):
        for dz, dc in ((1, 1), (0, 1), (1, 0), (0, 0)):
            if dc in cores:
                here = dz + dc == 0

                @pl.loop(int(here), 16, unroll=3 if here else 4)
                def _(p, dz=dz, dc=dc, here=here):
                    q = (p * 5 + (0 if here else 10)) & 15
                    x = (mx + (q >> 2)) & 3
                    y = (my + q) & 3
                    fn((((mz ^ dz) * 4 + x) * 4 + y) * 2 + (core ^ dc))

    loads = [
        pltpu.make_async_copy(src, dst, ld_sem.at[j])
        for j, (src, dst) in enumerate(
            (
                (wg_h, w_gate),
                (wo_h, w_out),
                (cot_h, cot_v),
                (in_h, in_v),
                (wi_h, w_in),
                (fa_h, fa),
                (ker_h, ker_v),
                (fb_h, fb),
            )
        )
    ]
    for cp in loads:
        cp.start()

    barrier = pltpu.get_barrier_semaphore()

    each_peer(
        lambda d: pl.semaphore_signal(barrier, inc=1, device_id=(d, te), device_id_type=MESH)
    )

    for q in range(1, TE):
        pl.semaphore_signal(
            barrier, inc=1, device_id=(me, lax.rem(te + q, TE)), device_id_type=MESH
        )

    def copy_to(src, dst, ph, device):
        return pltpu.make_async_remote_copy(
            src_ref=src,
            dst_ref=dst,
            send_sem=snd.at[ph],
            recv_sem=rcv.at[ph],
            device_id=device,
            device_id_type=MESH,
        )

    def send_all(slot_of, dst, ph):
        each_peer(lambda d: copy_to(slot_of(d), dst.at[me], ph, (d, te)).start())

    def wait_slots(ref, sem, slots=TM - 1):
        part = ref.at[pl.ds(0, slots)]
        pltpu.make_async_copy(part, part, sem).wait()

    for cp in loads[:4]:
        cp.wait()

    @pl.loop(0, N2 // CR)
    def _(c):
        for n in range(NB):
            gate = nn(four(in_v, c, n), w_gate[n])
            gg = nt(four(cot_v, c, n), w_out[n])
            put_four(gate_v, c, n, gate)
            put_four(gg_v, c, n, gg)
            so_g[pl.ds(c * DC, DC), :, lanes(n)] = (
                by_dest(gate * gg).astype(BF16).reshape(DC, LOC * KD, 128)
            )

    pl.semaphore_wait(barrier, TM - 1 + TE - 1)
    send_all(lambda d: so_g.at[d], rc_g, 0)

    loads[4].wait()
    loads[5].wait()
    for s in range(4):
        a_t[:, lanes(s)] = fa[lanes(s), :].T

    @pl.loop(0, LOC)
    def _(i):
        rows = pl.ds(pl.multiple_of(i * N2, N2), N2)
        for n in range(NB):
            mx_v[rows, lanes(n)] = nn(in_v[rows, lanes(n)], w_in[n]).astype(BF16)
        first_v[rows, :] = nn(a_t[...], mx_v[rows, :])

    loads[6].wait()

    @pl.loop(0, N2 // CR)
    def _(c):
        for n in range(NB):
            tw = four(first_v, c, n) * four(ker_v, c, n).astype(F32)
            so_f[pl.ds(c * DC, DC), :, lanes(n)] = (
                by_dest(tw).astype(BF16).reshape(DC, LOC * KD, 128)
            )

    send_all(lambda d: so_f.at[d], rc_f, 1)
    rc_g[me] = so_g[me]
    rc_f[me] = so_f[me]

    loads[7].wait()
    b_t[...] = fb[...].T

    @pl.loop(0, ROWS // 256)
    def _(c):
        rows = pl.ds(pl.multiple_of(c * 256, 256), 256)
        for n in range(NB):
            in_t[n, :, rows] = in_v[rows, lanes(n)].T
            cot_t[n, :, rows] = cot_v[rows, lanes(n)].T

    def columns(rc, x):
        @pl.loop(0, 8)
        def _(c):
            rows = pl.ds(pl.multiple_of(c * 256, 256), 256)
            for n in range(NB):
                xs[n, rows, :] = rc[pl.ds(c * 8, 8), :, lanes(n)].reshape(256, 128).astype(F32)

        for k in range(KD):
            for n in range(NB):
                x[k, :, lanes(n)] = xs[n, pl.ds(k, N1, stride=KD), :].astype(BF16)

    def product(lhs, x, slab):
        for k in range(KD):
            y = nn(lhs[...], x[k])
            for n in range(NB):
                xs[n, pl.ds(k, N1, stride=KD), :] = y[:, lanes(n)]

        @pl.loop(0, 8)
        def _(c):
            rows = pl.ds(pl.multiple_of(c * 256, 256), 256)
            for n in range(NB):
                slab(c, n)[...] = xs[n, rows, :].astype(BF16).reshape(8, LOC * KD, 128)

    wait_slots(rc_g, rcv.at[0])
    columns(rc_g, x_g)
    product(fb, x_g, lambda c, n: sr_g.at[pl.ds(c * 8, 8), :, lanes(n)])
    send_all(lambda d: sr_g.at[d], rr_g, 2)
    rr_g[me] = sr_g[me]

    wait_slots(rc_f, rcv.at[1])
    columns(rc_f, x_f)
    product(b_t, x_f, lambda c, n: sr_f.at[n, pl.ds(c * 8, 8)])
    for n in range(NB):
        send_all(lambda d, n=n: sr_f.at[n, d], rr_f.at[n], 3 + n)
    for n in range(NB):
        rr_f[n, me] = sr_f[n, me]

    fb_acc[...] = nt(x_f[0], x_g[0])

    @pl.loop(1, KD)
    def _(k):
        fb_acc[...] += nt(x_f[k], x_g[k])

    for h in range(2):
        r1s[:, h, :, 512:640] = fb_acc[:, lanes(h)].reshape(TM // 2, 8, 128)

    wait_slots(rr_g, rcv.at[2])

    @pl.loop(0, N2 // CR)
    def _(c):
        for n in range(NB):
            gt = by_block(
                rr_g[pl.ds(c * DC, DC), :, lanes(n)].reshape(LOC * CR, 128).astype(F32)
            )
            gf = (gt * four(ker_v, c, n).astype(F32)).astype(BF16)
            gk = (gt * four(first_v, c, n)).astype(BF16)
            put_four(gf_v, c, n, gf)
            put_four(gker_v, c, n, gk)

    fa_acc[...] = jnp.zeros_like(fa_acc)

    @pl.loop(0, LOC)
    def _(i):
        rows = pl.ds(pl.multiple_of(i * N2, N2), N2)
        gm_v[rows, :] = nn(fa[...], gf_v[rows, :]).astype(BF16)
        fa_acc[...] += nt(mx_v[rows, :], gf_v[rows, :])

    r1s[:, :, :, 0:512] = fa_acc[...].reshape(TM // 2, 2, 8, 512)
    for n in range(NB):
        r1s[n * 8 : (n + 1) * 8, :, :, 640:768] = nn(in_t[n], gm_v[:, lanes(n)]).reshape(
            8, 2, 8, 128
        )
    r1s[24:32, :, :, 640:768] = jnp.zeros((8, 2, 8, 128), F32)
    half = copy_to(r1s.at[:, 1 - core], rp, 9, (me ^ 1, te))
    half.start()

    def forward_tail(n):
        wait_slots(rr_f.at[n], rcv.at[3 + n])

        @pl.loop(0, N2 // CR)
        def _(c):
            sec = by_block(
                rr_f[n, pl.ds(c * DC, DC)].reshape(LOC * CR, 128).astype(F32)
            )
            put_four(gated_v, c, n, (sec * four(gate_v, c, n)).astype(BF16))
            put_four(ggate_v, c, n, (sec * four(gg_v, c, n)).astype(BF16))

        r2s[n, 0:16] = nn(in_t[n], ggate_v[:, lanes(n)]).reshape(16, 8, 128).astype(BF16)
        r2s[n, 16:32] = nn(cot_t[n], gated_v[:, lanes(n)]).T.reshape(16, 8, 128).astype(BF16)
        own = n % 2

        def send(d):
            @pl.when((d & 1) == own)
            def _():
                copy_to(r2s.at[n, d >> 1], r2r.at[n, me], 11 + n, (d, te)).start()

        each_peer(send)

        @pl.when(core == own)
        def _():
            r2r[n, me] = r2s[n, chip]

    forward_tail(0)
    half.wait_recv()

    @pl.loop(0, TM // 2)
    def _(g):
        both = rp[g] + r1s[g, core]
        r1b[g] = jnp.concatenate([both[:, 0:CH], both[:, CH:]], axis=0).astype(BF16)

    each_peer(
        lambda d: copy_to(r1b.at[d >> 1], r1r.at[chip], 6, (d, te)).start(), cores=(0,)
    )
    r1r[chip] = r1b[chip]
    forward_tail(1)
    forward_tail(2)

    @pl.loop(0, ROWS // 256)
    def _(c):
        rows = pl.ds(pl.multiple_of(c * 256, 256), 256)
        for n in range(NB):
            out_v[rows, lanes(n)] = nn(gated_v[rows, lanes(n)], w_out[n]).astype(BF16)
            gin_v[rows, lanes(n)] = (
                nt(gm_v[rows, lanes(n)], w_in[n]) + nt(ggate_v[rows, lanes(n)], w_gate[n])
            ).astype(BF16)

    def four_slots(q):
        a, b, c, d = (r1r[q * 4 + j].astype(F32) for j in range(4))
        return (a + b) + (c + d)

    token_scale = 1.0 / math.sqrt(N1 * N2)
    wait_slots(r1r, rcv.at[6], TM // 2 - 1)
    sum1 = lax.fori_loop(0, TM // 8, lambda q, acc: acc + four_slots(q), jnp.zeros((16, CH), F32))
    tr[te, :, 0:CH] = sum1[0:8]
    tr[te, :, CH:640] = sum1[8:16, 0:256]
    for q in range(1, TE):
        copy_to(tr.at[te], tr.at[te], 7, (me, lax.rem(te + q, TE))).start()

    def to_chips(piece, ph):
        each_peer(lambda d: copy_to(piece, piece, ph, (d, te)).start(), cores=(0,))

    @pl.when(me < OWN)
    def _():
        ag1[chip, core] = sum1[8:16, 256:CH] * token_scale
        to_chips(ag1.at[chip, core], 10)

    for n in range(NB):

        @pl.when(core == n % 2)
        def _(n=n):
            wait_slots(r2r.at[n], rcv.at[11 + n])
            ag2[n, chip] = jnp.sum(r2r[n].astype(F32), axis=0) * token_scale
            if n < NB - 1:
                to_chips(ag2.at[n, chip], 14 + n)
            else:
                piece = ag2.at[n, chip]
                each_peer(lambda d: copy_to(piece, piece, 14 + n, (d, te)).start())

    wait_slots(tr, rcv.at[7], TE - 1)
    total = tr[0] + tr[1] + tr[2] + tr[3]
    gfa[...] = total[:, 0:512] * (1.0 / math.sqrt(N1 * D))
    pr[core] = total[:, 512:640] * (1.0 / math.sqrt(N2 * D))
    pair = copy_to(pr.at[core], pr.at[core], 8, (me ^ 1, te))
    pair.start()

    def either(cond, then, other):
        @pl.when(cond)
        def _():
            then()

        @pl.when(jnp.logical_not(cond))
        def _():
            other()

    other = (me ^ 1, te)
    either(
        me < OWN,
        lambda: wait_slots(ag2.at[0], rcv.at[10], OWN // 2 - 1),
        lambda: wait_slots(ag2.at[0], rcv.at[10], OWN // 2),
    )
    pass1 = copy_to(ag1.at[:, core], ag1.at[:, core], 17, other)
    pass1.start()
    for n in range(NB - 1):

        @pl.when(core == n % 2)
        def _(n=n):
            wait_slots(ag2.at[n], rcv.at[14 + n], TM // 2 - 1)
            copy_to(ag2.at[n], ag2.at[n], 18 + n, other).start()

    pair.wait()
    for h in range(2):
        gfb[:, lanes(h)] = jnp.where(core == 0, pr[h, 0:4, :], pr[h, 4:8, :])

    pass1.wait_recv()
    gw_in[...] = ag1[...].reshape(OWN, 8, 128)
    for n in range(NB):

        if n < NB - 1:

            @pl.when(core != n % 2)
            def _(n=n):
                wait_slots(ag2.at[n], rcv.at[18 + n], TM // 2)

        else:
            either(
                core == n % 2,
                lambda: wait_slots(ag2.at[n], rcv.at[14 + n], TM // 2 - 1),
                lambda: wait_slots(ag2.at[n], rcv.at[14 + n], TM // 2),
            )
        gw_gate[n * 16 : (n + 1) * 16] = ag2[n, 0:16]
        gw_out[n * 16 : (n + 1) * 16] = ag2[n, 16:32]

    wait_slots(rc_g, snd.at[0])
    wait_slots(rc_f, snd.at[1])
    wait_slots(rr_g, snd.at[2])
    for n in range(NB):
        wait_slots(rr_f.at[n], snd.at[3 + n])
        either(
            core == n % 2,
            lambda: wait_slots(r2r.at[n], snd.at[11 + n], TM // 2 - 1),
            lambda: wait_slots(r2r.at[n], snd.at[11 + n], TM // 2),
        )

        @pl.when(core == n % 2)
        def _(n=n):
            if n < NB - 1:
                wait_slots(ag2.at[n], snd.at[14 + n], TM // 2 - 1)
                wait_slots(ag2.at[n], snd.at[18 + n], TM // 2)
            else:
                wait_slots(ag2.at[n], snd.at[14 + n], TM // 2)
                wait_slots(ag2.at[n], snd.at[14 + n], TM // 2 - 1)

    wait_slots(r1r, snd.at[6], TM // 2 - 1)
    wait_slots(tr, snd.at[7], TE - 1)
    half.wait_send()
    pass1.wait_send()

    @pl.when(me < OWN)
    def _():
        wait_slots(ag2.at[0], snd.at[10], TM // 2 - 1)


def finish_body(*refs):
    srcs, dsts, sem = refs[:8], refs[8:16], refs[16]
    stores = []
    for src, dst in zip(srcs, dsts, strict=True):
        cuts = 4 if src.shape[0] == ROWS else 1
        step = src.shape[0] // cuts
        for j in range(cuts):
            rows = pl.ds(j * step, step)
            stores.append(pltpu.make_async_copy(src.at[rows], dst.at[rows], sem.at[len(stores)]))
    for cp in stores:
        cp.start()
    for cp in stores:
        cp.wait()


def body(inputs, kernel, w_in, w_gate, w_out, factor_a, factor_b, cotangent):
    any_spec = pl.BlockSpec(memory_space=pl.ANY)
    vm = pl.BlockSpec(memory_space=pltpu.VMEM)
    wide = pltpu.VMEM((ROWS, CH), F32)
    act = pltpu.VMEM((ROWS, CH), BF16)
    turned = pltpu.VMEM((NB, 128, ROWS), BF16)
    slots = pltpu.VMEM((TM, LOC * KD, CH), BF16)
    mixer = pltpu.VMEM((NB, 128, 128), BF16)
    slots_n = pltpu.VMEM((NB, TM, LOC * KD, 128), BF16)
    cols = pltpu.VMEM((KD, N1, CH), BF16)
    tile = pltpu.VMEM((OWN, 8, 128), F32)
    outs = pl.pallas_call(
        kernel_body,
        name="monarch",
        out_shape=(
            act,
            act,
            act,
            tile,
            tile,
            tile,
            pltpu.VMEM((8, N2), F32),
            pltpu.VMEM((4, N1), F32),
        ),
        in_specs=[any_spec] * 8,
        out_specs=(vm,) * 8,
        scratch_shapes=[
            act,
            act,
            act,
            mixer,
            mixer,
            mixer,
            pltpu.VMEM((N2, N2), BF16),
            pltpu.VMEM((N1, N1), BF16),
            turned,
            turned,
            pltpu.VMEM((N2, N2), BF16),
            pltpu.VMEM((N1, N1), BF16),
            wide,
            wide,
            wide,
            act,
            slots,
            slots,
            slots,
            slots,
            pltpu.VMEM((NB, ROWS, 128), F32),
            cols,
            cols,
            slots,
            slots_n,
            slots,
            slots_n,
            act,
            act,
            act,
            act,
            pltpu.VMEM((N1, N1), F32),
            pltpu.VMEM((N2, N2), F32),
            pltpu.VMEM((TM // 2, 2, 8, 768), F32),
            pltpu.VMEM((TM // 2, 16, CH), BF16),
            pltpu.VMEM((TM // 2, 16, CH), BF16),
            pltpu.VMEM((TM // 2, 8, 768), F32),
            pltpu.VMEM((NB, TM // 2, 8, 128), BF16),
            pltpu.VMEM((NB, TM, 8, 128), BF16),
            pltpu.VMEM((TE, 8, 640), F32),
            pltpu.VMEM((2, 8, 128), F32),
            pltpu.VMEM((OWN // 2, 2, 8, 128), F32),
            pltpu.VMEM((NB, TM // 2, 8, 128), F32),
            pltpu.SemaphoreType.DMA((8,)),
            pltpu.SemaphoreType.DMA((21,)),
            pltpu.SemaphoreType.DMA((21,)),
        ],
        compiler_params=pltpu.CompilerParams(
            collective_id=0, has_side_effects=True, vmem_limit_bytes=57 << 20
        ),
    )(inputs, kernel, w_in, w_gate, w_out, factor_a, factor_b, cotangent)
    outs = pl.pallas_call(
        finish_body,
        name="finish",
        out_shape=tuple(jax.ShapeDtypeStruct(o.shape, o.dtype) for o in outs),
        in_specs=[vm] * len(outs),
        out_specs=(any_spec,) * len(outs),
        scratch_shapes=[pltpu.SemaphoreType.DMA((17,))],
        compiler_params=pltpu.CompilerParams(vmem_limit_bytes=8 << 20),
    )(*outs)
    out, gin, gker, gwi, gwg, gwo, gfa, gfb = outs
    shape = (NB, 128, 128)
    return (
        out,
        gin,
        gker,
        gwi.reshape(shape),
        gwg.reshape(shape),
        gwo.reshape(shape),
        gfa,
        gfb,
    )


def solution(mesh):
    return jax.shard_map(
        body,
        mesh=mesh,
        in_specs=(
            P("tm", "tensor"),
            P("tm", "tensor"),
            P("tensor", None, None),
            P("tensor", None, None),
            P("tensor", None, None),
            P(),
            P(),
            P("tm", "tensor"),
        ),
        out_specs=(
            P("tm", "tensor"),
            P("tm", "tensor"),
            P("tm", "tensor"),
            P("tensor", None, None),
            P("tensor", None, None),
            P("tensor", None, None),
            P("tm", None),
            P("tm", None),
        ),
        check_vma=False,
    )
```
